128 devices in a mesh: dx: 8 (over z, core), dy: 16 (over x, y).
Axes of the slice: x: 4, y: 4, z: 4, core: 2. Of those that a mesh axis runs over, the one named last changes fastest.
Arguments:
- dust: bfloat16 [524288, 256], P(('dx', 'dy')), may hold values from 0.19921875 to 2
- classes: int32 [524288], P(('dx', 'dy')), may hold values from 0 to 7
- kernels: bfloat16 [8, 2, 128, 128], replicated, may hold values from -0.5 to 0.5
- export_ids: int32 [128, 4, 1024], P(('dx', 'dy')), may hold values from 0 to 4095
- faces: int32 [6, 524288], P(None, ('dx', 'dy')), may hold values from 0 to 8191, as said below
- face_coef: float32 [6, 524288], P(None, ('dx', 'dy')), may hold values from 0.04 to 0.16
- mig_ids: int32 [16384, 16], P(('dx', 'dy')), may hold values from 0 to 4095, as said below
- mig_counts: int32 [128, 128], P(('dx', 'dy')), may hold values from 0 to 16, as said below
Outputs:
- dust_next: bfloat16 [524288, 256], P(('dx', 'dy'))
- arrivals: bfloat16 [262144, 256], P(('dx', 'dy'))
The draws below stay inside these ranges and needn't reach their ends.
Inputs may be any that keep to these rules, and one draw needn't show every extreme that they name: Entries below 4096 name cells of the same domain, entries from 4096 on name its received rows in the order of the steps; each cell has 4 to 6 faces and its other slots name the cell itself. `mig_ids`: the 2048 entries of one domain's rows are distinct local cells. `mig_counts`: one destination, drawn from the seed, receives 16 cells from every domain.
All inputs are finite; a program needn't handle non-finite values.
Results may differ from the reference program's by a relative error of at most 0.0054.
Values may be sent and summed in bfloat16 or wider, within the bound.
A program may use at most 64 MiB of HBM per device.

```python
import math
import jax
import jax.numpy as jnp
from jax import lax

B = 128
S = 2
NCLASS = 8
NFACE = 6
SUBSTEPS = 6
CAP = 16
CELLS_DEV = 4096
EXP = 1024
NDEV = 128
CELLS = 524288
N_DX = 8
N_DY = 16


def draw_faces(key, part):
    key_count, key_local, key_ghost, key_choose = jax.random.split(key, 4)
    own_index = jnp.arange(CELLS, dtype=jnp.int32) % CELLS_DEV
    real_count = jax.random.randint(key_count, (CELLS,), 4, NFACE + 1)
    slot_number = jnp.arange(NFACE, dtype=jnp.int32)[:, None]
    local_target = jax.random.randint(key_local, (NFACE, CELLS), 0, CELLS_DEV)
    ghost_target = CELLS_DEV + jax.random.randint(key_ghost, (NFACE, CELLS), 0, 4 * EXP)
    chooser = jax.random.randint(key_choose, (NFACE, CELLS), 0, 10)
    target = jnp.where(chooser == 0, ghost_target, local_target)
    return jnp.where(slot_number < real_count[None, :], target, own_index[None, :]).astype(jnp.int32)


def draw_mig_ids(key, part):
    domain_keys = jax.random.split(key, NDEV)

    def permuted(domain_key):
        return jax.random.permutation(domain_key, CELLS_DEV)[:NDEV * CAP].astype(jnp.int32)
    return jax.vmap(permuted)(domain_keys).reshape(NDEV * NDEV, CAP)


def draw_mig_counts(key, part):
    key_base, key_target = jax.random.split(key)
    base_counts = jax.random.randint(key_base, (NDEV, NDEV), 0, CAP + 1)
    busiest = jax.random.randint(key_target, (), 0, NDEV)
    column = jnp.arange(NDEV, dtype=jnp.int32)[None, :]
    return jnp.where(column == busiest, CAP, base_counts).astype(jnp.int32)


def touch_ends(drawn, key, smallest, top_value):
    index_at = [jax.random.randint(jax.random.fold_in(key, axis), (), 0, length) for axis, length in enumerate(drawn.shape)]
    widest = drawn.shape.index(max(drawn.shape))
    beside = index_at[:widest] + [(index_at[widest] + 1) % drawn.shape[widest]] + index_at[widest + 1:]
    return drawn.at[tuple(index_at)].set(smallest).at[tuple(beside)].set(top_value)


def block_levels(key, shape, cuts, least, high):
    def one(axis_at, parts):
        draws = jax.random.uniform(jax.random.fold_in(jax.random.fold_in(key, 6), axis_at), (parts,), jnp.float32, least / len(cuts), high / len(cuts))
        return jnp.repeat(jnp.exp(draws), shape[axis_at] // parts).reshape((-1,) + (1,) * (len(shape) - axis_at - 1))

    level = one(*cuts[0])
    for cut in cuts[1:]:
        level = level * one(*cut)
    return level


def scatter_about(rng, extent, scale, limit, kind=jnp.bfloat16):
    result = scale * jax.random.normal(rng, extent, jnp.float32)
    return jnp.clip(result, min=-limit, max=limit).astype(kind)


def setup_inputs(seed: int = 0) -> dict:
    seeds = jax.random.split(jax.random.key(seed), 9)
    dust = jnp.clip(0.19921875 + 1.8007812 * jax.random.uniform(seeds[0], (CELLS, S * B), jnp.float32) ** block_levels(seeds[0], (CELLS, S * B), ((0, 128),), -0.2, 0.2), 0.19921875, 2.0).astype(jnp.bfloat16)
    classes = touch_ends(jax.random.randint(seeds[1], (CELLS,), 0, NCLASS), jax.random.fold_in(seeds[1], 1), 0, NCLASS - 1).astype(jnp.int32)
    kernels = scatter_about(seeds[2], (NCLASS, S, B, B), B ** -0.5, 0.5)
    export_ids = touch_ends(jax.random.randint(seeds[3], (NDEV, 4, EXP), 0, CELLS_DEV), jax.random.fold_in(seeds[3], 1), 0, CELLS_DEV - 1).astype(jnp.int32)
    faces = draw_faces(jax.random.fold_in(seeds[8], 71), 0)
    face_coef = jnp.clip(jnp.exp(math.log(0.16) - 1.3862944 * jax.random.uniform(seeds[5], (NFACE, CELLS), jnp.float32) ** block_levels(seeds[5], (NFACE, CELLS), ((1, 128),), -0.2, 0.2)), 0.04, 0.16)
    mig_ids = draw_mig_ids(jax.random.fold_in(seeds[8], 71), 0)
    mig_counts = draw_mig_counts(jax.random.fold_in(seeds[8], 71), 0)
    return dict(dust=dust, classes=classes, kernels=kernels, export_ids=export_ids, faces=faces, face_coef=face_coef, mig_ids=mig_ids, mig_counts=mig_counts)


def coagulate(dust_rows, dust_classes, kernels):
    row_count = dust_rows.shape[0]
    sort_order = jnp.argsort(dust_classes, stable=True).astype(jnp.int32)
    sorted_rows = jnp.take(dust_rows, sort_order, axis=0)
    sorted_classes = jnp.take(dust_classes, sort_order, axis=0)
    block_rows = 2048 if row_count % 2048 == 0 else row_count
    block_count = row_count // block_rows

    def run_block(pieces):
        piece_rows, piece_classes = pieces
        lowest = piece_classes[0]
        highest = piece_classes[block_rows - 1]
        grain_state = piece_rows.astype(jnp.float32).reshape(block_rows, S, B)
        for substep in range(SUBSTEPS):
            operand = lax.optimization_barrier(grain_state.astype(jnp.bfloat16)).astype(jnp.float32)

            def add_class(class_id, product):
                kernel = lax.dynamic_index_in_dim(kernels, class_id, 0, keepdims=False).astype(jnp.float32)
                partial_value = jnp.einsum("rsb,sbc->rsc", operand, kernel)
                return jnp.where((piece_classes == class_id)[:, None, None], partial_value, product)

            product = lax.fori_loop(lowest, highest + 1, add_class, jnp.zeros((block_rows, S, B), jnp.float32))
            mean_square = jnp.mean(grain_state * grain_state, axis=2, keepdims=True)
            grain_state = grain_state + product * (mean_square / (1.0 + mean_square))
        return grain_state.reshape(block_rows, S * B).astype(jnp.bfloat16)

    blocked = lax.map(run_block, (sorted_rows.reshape(block_count, block_rows, S * B), sorted_classes.reshape(block_count, block_rows)))
    inverse = jnp.zeros((row_count,), jnp.int32).at[sort_order].set(jnp.arange(row_count, dtype=jnp.int32))
    return jnp.take(blocked.reshape(row_count, S * B), inverse, axis=0)


def reference(dust, classes, kernels, export_ids, faces, face_coef, mig_ids, mig_counts):
    devices = N_DX * N_DY
    cells_local = dust.shape[0] // devices
    row_width = S * B
    coag = coagulate(dust, classes, kernels)
    domain_rows = coag.reshape(N_DX, N_DY, cells_local, row_width)
    export_rows = export_ids.reshape(N_DX, N_DY, 4 * EXP)

    def pick_rows(source, index):
        return jnp.take(source, index, axis=0)

    outbound = jax.vmap(jax.vmap(pick_rows))(domain_rows, export_rows).reshape(N_DX, N_DY, 4, EXP, row_width)
    ghosts = jnp.stack([
        jnp.roll(outbound[:, :, 0], 1, axis=0),
        jnp.roll(outbound[:, :, 1], -1, axis=0),
        jnp.roll(outbound[:, :, 2], 1, axis=1),
        jnp.roll(outbound[:, :, 3], -1, axis=1)], axis=2).reshape(N_DX, N_DY, 4 * EXP, row_width)
    extended = jnp.concatenate([domain_rows, ghosts], axis=2).reshape(devices, cells_local + 4 * EXP, row_width)
    local_faces = faces.reshape(NFACE, devices, cells_local).transpose(1, 0, 2)
    local_coefs = face_coef.reshape(NFACE, devices, cells_local).transpose(1, 0, 2)

    def diffuse(pieces):
        extended_rows, face_rows, coefs = pieces
        own_rows = extended_rows[:cells_local].astype(jnp.float32)
        flux_sum = own_rows
        for face in range(NFACE):
            neighbour = jnp.take(extended_rows, face_rows[face], axis=0).astype(jnp.float32)
            flux_sum = flux_sum + coefs[face][:, None] * (neighbour - own_rows)
        return flux_sum.astype(jnp.bfloat16)

    updated = lax.map(diffuse, (extended, local_faces, local_coefs))
    slot_index = mig_ids.reshape(devices, devices, CAP)
    filled = jnp.arange(CAP, dtype=jnp.int32)[None, None, :] < mig_counts[:, :, None]

    def pack(pieces):
        source_rows, index, valid = pieces
        picked = jnp.take(source_rows, index.reshape(devices * CAP), axis=0).reshape(devices, CAP, row_width)
        return jnp.where(valid[:, :, None], picked, jnp.zeros_like(picked))

    leaving = lax.map(pack, (updated, slot_index, filled))
    arrivals = leaving.transpose(1, 0, 2, 3).reshape(devices * devices * CAP, row_width)
    return updated.reshape(devices * cells_local, row_width), arrivals
```

```python
import functools
import jax
import jax.numpy as jnp
from jax import lax
from jax.experimental import pallas as pl
from jax.experimental.pallas import tpu as pltpu
from jax.sharding import PartitionSpec as P

SUBSTEPS = 6
MESH = pl.DeviceIdType.MESH
f32, bf16, i32, i16 = jnp.float32, jnp.bfloat16, jnp.int32, jnp.int16
LANES = 128
CHUNK = 1024


def column(row):
    return jnp.broadcast_to(row, (LANES, LANES)).T


def interleave(wide, first, block):
    n = block.shape[0]
    wide[pl.ds(2 * first, n, stride=2), :] = block[:, :LANES]
    wide[pl.ds(2 * first + 1, n, stride=2), :] = block[:, LANES:]


def merged(wide, first, n):
    left = wide[pl.ds(2 * first, n, stride=2), :]
    right = wide[pl.ds(2 * first + 1, n, stride=2), :]
    return jnp.concatenate([left, right], axis=1)


def coag_kernel(blocks, cls_ref, dust_ref, ker_ref, ids_ref, coag_ref, out_ref, wide, picked, cls_wide, *rest):
    ids, sem = rest[:4], rest[4]
    step = pl.program_id(0)
    rows = dust_ref.shape[0]
    copies = [
        pltpu.make_async_copy(ids_ref.at[pl.ds(k * CHUNK, CHUNK)], ids[k], sem.at[k]) for k in range(4)
    ]

    @pl.when(step == 0)
    def _():
        for copy in copies:
            copy.start()

    for k in range(rows // LANES):
        cls_wide[k * LANES:(k + 1) * LANES, :] = column(cls_ref[k:k + 1, :])
    group = cls_wide[...]
    pair = (group >> 1).astype(i16)
    odd = (group & 1) == 1
    masks = [pair == p for p in range(4)]
    block = dust_ref[...].astype(f32)
    state = [block[:, :LANES], block[:, LANES:]]
    for substep in range(SUBSTEPS):
        following = []
        for s in range(2):
            operand = state[s].astype(bf16)
            zero = jnp.zeros_like(operand)
            spread = jnp.concatenate([jnp.where(m, operand, zero) for m in masks], axis=1)
            weights = jnp.concatenate(
                [jnp.concatenate([ker_ref[2 * p, s], ker_ref[2 * p + 1, s]], axis=1) for p in range(4)], axis=0
            )
            both = jnp.dot(spread, weights, preferred_element_type=f32)
            product = jnp.where(odd, both[:, LANES:], both[:, :LANES])
            mean_square = jnp.mean(state[s] * state[s], axis=1, keepdims=True)
            following.append(state[s] + product * (mean_square / (1.0 + mean_square)))
        state = following
    rounded = jnp.concatenate(state, axis=1).astype(bf16)
    coag_ref[...] = rounded
    interleave(wide, step * rows, rounded.astype(f32))

    @pl.when(step == blocks - 1)
    def _():
        for copy in copies:
            copy.wait()

        def pick(i, carry):
            for v in range(4):
                at = i * 4 + v
                for k in range(4):
                    row = pl.multiple_of(ids[k][at], 2)
                    picked[pl.ds(pl.multiple_of(2 * (k * CHUNK) + 2 * at, 2), 2), :] = wide[pl.ds(row, 2), :]
            return carry

        lax.fori_loop(0, CHUNK // 4, pick, 0)

        def narrow(i, carry):
            first = pl.multiple_of(i * 256, 256)
            out_ref[pl.ds(first, 256), :] = merged(picked, first, 256).astype(bf16)
            return carry

        lax.fori_loop(0, 4 * CHUNK // 256, narrow, 0)


def coagulate(dust, classes, kernels, export_flat):
    rows = dust.shape[0]
    block = 1024
    blocks = rows // block
    return pl.pallas_call(
        functools.partial(coag_kernel, blocks),
        grid=(blocks,),
        in_specs=[
            pl.BlockSpec((block // LANES, LANES), lambda i: (i, 0)),
            pl.BlockSpec((block, 256), lambda i: (i, 0)),
            pl.BlockSpec(kernels.shape, lambda i: (0, 0, 0, 0)),
            pl.BlockSpec(memory_space=pl.ANY),
        ],
        out_specs=[
            pl.BlockSpec((block, 256), lambda i: (i, 0)),
            pl.BlockSpec((4 * CHUNK, 256), lambda i: (0, 0)),
        ],
        out_shape=[
            jax.ShapeDtypeStruct((rows, 256), bf16),
            jax.ShapeDtypeStruct((4 * CHUNK, 256), bf16),
        ],
        scratch_shapes=[
            pltpu.VMEM((2 * rows, LANES), f32),
            pltpu.VMEM((8 * CHUNK, LANES), f32),
            pltpu.VMEM((block, LANES), i32),
            *[pltpu.SMEM((CHUNK,), i32)] * 4,
            pltpu.SemaphoreType.DMA((4,)),
        ],
        compiler_params=pltpu.CompilerParams(vmem_limit_bytes=56 << 20),
        name="coagulate",
    )(classes.reshape(rows // LANES, LANES), dust, kernels, export_flat)


def exchange_kernel(n_dx, n_dy, out_ref, ghost_ref, send_sem, recv_sem):
    a, b = lax.axis_index("dx"), lax.axis_index("dy")
    peers = [
        (lax.rem(a + 1, n_dx), b),
        (lax.rem(a + n_dx - 1, n_dx), b),
        (a, lax.rem(b + 1, n_dy)),
        (a, lax.rem(b + n_dy - 1, n_dy)),
    ]
    barrier = pltpu.get_barrier_semaphore()
    for peer in peers:
        pl.semaphore_signal(barrier, inc=1, device_id=peer, device_id_type=MESH)
    pl.semaphore_wait(barrier, 4)
    copies = []
    for k in (2, 3, 0, 1):
        copy = pltpu.make_async_remote_copy(
            src_ref=out_ref.at[pl.ds(k * CHUNK, CHUNK)],
            dst_ref=ghost_ref.at[pl.ds(k * CHUNK, CHUNK)],
            send_sem=send_sem.at[k],
            recv_sem=recv_sem.at[k],
            device_id=peers[k],
            device_id_type=MESH,
        )
        copy.start()
        copies.append(copy)
    for copy in copies:
        copy.wait()


def exchange(outbound, n_dx, n_dy):
    return pl.pallas_call(
        functools.partial(exchange_kernel, n_dx, n_dy),
        in_specs=[pl.BlockSpec(memory_space=pl.ANY)],
        out_specs=pl.BlockSpec(memory_space=pl.ANY),
        out_shape=jax.ShapeDtypeStruct(outbound.shape, outbound.dtype),
        scratch_shapes=[pltpu.SemaphoreType.DMA((4,)), pltpu.SemaphoreType.DMA((4,))],
        compiler_params=pltpu.CompilerParams(collective_id=0, has_side_effects=True),
        name="exchange",
    )(outbound)


FACES = 6
SPLIT = 4
UNROLL = 4


def diffuse_kernel(coag_ref, ghost_ref, coef_ref, faces_ref, mig_ref, count_ref, next_ref, leave_ref,
                   ext, coefs, wide, picked, *rest):
    ids, migs, sem = rest[:SPLIT * FACES], rest[SPLIT * FACES:SPLIT * FACES + 2], rest[-1]
    rows = coag_ref.shape[0]
    copies = []
    for f in range(FACES):
        for u in range(SPLIT):
            k = f * SPLIT + u
            copies.append(pltpu.make_async_copy(
                faces_ref.at[pl.ds(f * rows + u * CHUNK, CHUNK)], ids[k], sem.at[k]))
    for m in range(2):
        copies.append(pltpu.make_async_copy(
            mig_ref.at[pl.ds(m * CHUNK, CHUNK)], migs[m], sem.at[SPLIT * FACES + m]))
    for copy in copies:
        copy.start()

    def widen(i, carry):
        first = pl.multiple_of(i * 128, 128)
        interleave(ext, first, coag_ref[pl.ds(first, 128), :].astype(f32))
        interleave(ext, rows + first, ghost_ref[pl.ds(first, 128), :].astype(f32))
        return carry

    lax.fori_loop(0, rows // 128, widen, 0)

    def spread(i, carry):
        first = pl.multiple_of(i * LANES, LANES)
        block = coef_ref[:, pl.ds(first, LANES)]
        for f in range(FACES):
            coefs[pl.ds(pl.multiple_of(f * rows + first, LANES), LANES), :] = column(block[f:f + 1, :])
        kept = 1.0 - jnp.sum(block, axis=0, keepdims=True)
        coefs[pl.ds(pl.multiple_of(FACES * rows + first, LANES), LANES), :] = column(kept)
        return carry

    lax.fori_loop(0, rows // LANES, spread, 0)
    for copy in copies:
        copy.wait()

    def step(i, carry):
        for v in range(UNROLL):
            at = i * UNROLL + v
            for u in range(SPLIT):
                cell = u * CHUNK + at
                total = ext[pl.ds(pl.multiple_of(2 * cell, 2), 2), :] * coefs[
                    pl.ds(FACES * rows + cell, 2, stride=0), :]
                for f in range(FACES):
                    row = pl.multiple_of(ids[f * SPLIT + u][at], 2)
                    total = total + ext[pl.ds(row, 2), :] * coefs[pl.ds(f * rows + cell, 2, stride=0), :]
                wide[pl.ds(pl.multiple_of(2 * cell, 2), 2), :] = total
        return carry

    lax.fori_loop(0, CHUNK // UNROLL, step, 0)

    def narrow(i, carry):
        first = pl.multiple_of(i * 256, 256)
        next_ref[pl.ds(first, 256), :] = merged(wide, first, 256).astype(bf16)
        return carry

    lax.fori_loop(0, rows // 256, narrow, 0)

    def pick(i, carry):
        for v in range(8):
            at = i * 8 + v
            for m in range(2):
                row = pl.multiple_of(migs[m][at], 2)
                picked[pl.ds(pl.multiple_of(2 * (m * CHUNK) + 2 * at, 2), 2), :] = wide[pl.ds(row, 2), :]
        return carry

    lax.fori_loop(0, CHUNK // 8, pick, 0)
    slot = lax.broadcasted_iota(i32, (16, 256), 0)

    def leave(i, carry):
        for v in range(8):
            domain = i * 8 + v
            first = pl.multiple_of(domain * 16, 16)
            block = merged(picked, first, 16)
            leave_ref[pl.ds(first, 16), :] = jnp.where(slot < count_ref[domain], block, 0.0).astype(bf16)
        return carry

    lax.fori_loop(0, leave_ref.shape[0] // 128, leave, 0)


def diffuse(coag, ghosts, face_coef, faces_flat, mig_flat, counts):
    rows = coag.shape[0]
    vmem = pl.BlockSpec(memory_space=pltpu.VMEM)
    hbm = pl.BlockSpec(memory_space=pl.ANY)
    return pl.pallas_call(
        diffuse_kernel,
        in_specs=[vmem, vmem, vmem, hbm, hbm, pl.BlockSpec(memory_space=pltpu.SMEM)],
        out_specs=[vmem, vmem],
        out_shape=[
            jax.ShapeDtypeStruct((rows, 256), bf16),
            jax.ShapeDtypeStruct((2 * CHUNK, 256), bf16),
        ],
        scratch_shapes=[
            pltpu.VMEM((4 * rows, LANES), f32),
            pltpu.VMEM(((FACES + 1) * rows, LANES), f32),
            pltpu.VMEM((2 * rows, LANES), f32),
            pltpu.VMEM((4 * CHUNK, LANES), f32),
            *[pltpu.SMEM((CHUNK,), i32)] * (SPLIT * FACES + 2),
            pltpu.SemaphoreType.DMA((SPLIT * FACES + 2,)),
        ],
        compiler_params=pltpu.CompilerParams(vmem_limit_bytes=56 << 20),
        name="diffuse",
    )(coag, ghosts, face_coef, faces_flat, mig_flat, counts)


def migrate_kernel(n_dx, n_dy, leave_ref, arrive_ref, send_sem, recv_sem, own_sem):
    a, b = lax.axis_index("dx"), lax.axis_index("dy")
    me = a * n_dy + b
    count = n_dx * n_dy
    cap = leave_ref.shape[0] // count

    def greet(k, carry):
        peer = lax.rem(me + k, count)
        pl.semaphore_signal(
            pltpu.get_barrier_semaphore(), inc=1, device_id=(peer // n_dy, lax.rem(peer, n_dy)), device_id_type=MESH)
        return carry

    lax.fori_loop(1, count, greet, 0)
    pl.semaphore_wait(pltpu.get_barrier_semaphore(), count - 1)

    def block(peer):
        return pl.ds(pl.multiple_of(peer * cap, cap), cap)

    def remote(k):
        peer = lax.rem(me + k, count)
        return pltpu.make_async_remote_copy(
            src_ref=leave_ref.at[block(peer)],
            dst_ref=arrive_ref.at[block(me)],
            send_sem=send_sem.at[k],
            recv_sem=recv_sem.at[k],
            device_id=(peer // n_dy, lax.rem(peer, n_dy)),
            device_id_type=MESH,
        )

    own = pltpu.make_async_copy(leave_ref.at[block(me)], arrive_ref.at[block(me)], own_sem)
    own.start()

    def send(k, carry):
        remote(k).start()
        return carry

    lax.fori_loop(1, count, send, 0)
    own.wait()

    def finish(k, carry):
        remote(k).wait()
        return carry

    lax.fori_loop(1, count, finish, 0)


def migrate(leaving, n_dx, n_dy):
    count = n_dx * n_dy
    return pl.pallas_call(
        functools.partial(migrate_kernel, n_dx, n_dy),
        in_specs=[pl.BlockSpec(memory_space=pl.ANY)],
        out_specs=pl.BlockSpec(memory_space=pl.ANY),
        out_shape=jax.ShapeDtypeStruct(leaving.shape, leaving.dtype),
        scratch_shapes=[
            pltpu.SemaphoreType.DMA((count,)), pltpu.SemaphoreType.DMA((count,)), pltpu.SemaphoreType.DMA],
        compiler_params=pltpu.CompilerParams(collective_id=1, has_side_effects=True),
        name="migrate",
    )(leaving)


def body(n_dx, n_dy, dust, classes, kernels, export_ids, faces, face_coef, mig_ids, mig_counts):
    coag, outbound = coagulate(dust, classes, kernels, (export_ids * 2).reshape(-1))
    ghosts = exchange(outbound, n_dx, n_dy)
    updated, leaving = diffuse(
        coag, ghosts, face_coef, (faces * 2).reshape(-1), (mig_ids * 2).reshape(-1), mig_counts.reshape(-1))
    return updated, migrate(leaving, n_dx, n_dy)


def solution(mesh):
    return jax.shard_map(
        functools.partial(body, mesh.shape["dx"], mesh.shape["dy"]),
        mesh=mesh,
        in_specs=(
            P(("dx", "dy"), None),
            P(("dx", "dy")),
            P(),
            P(("dx", "dy"), None, None),
            P(None, ("dx", "dy")),
            P(None, ("dx", "dy")),
            P(("dx", "dy"), None),
            P(("dx", "dy"), None),
        ),
        out_specs=(P(("dx", "dy"), None), P(("dx", "dy"), None)),
        check_vma=False,
    )
```

```python
import functools
import jax
import jax.numpy as jnp
from jax import lax
from jax.experimental import pallas as pl
from jax.experimental.pallas import tpu as pltpu
from jax.sharding import PartitionSpec as P

SUBSTEPS = 6
MESH = pl.DeviceIdType.MESH
f32, bf16, i32, i16 = jnp.float32, jnp.bfloat16, jnp.int32, jnp.int16
LANES = 128
CHUNK = 1024


def column(row):
    return jnp.broadcast_to(row, (LANES, LANES)).T


def interleave(wide, first, block):
    n = block.shape[0]
    wide[pl.ds(2 * first, n, stride=2), :] = block[:, :LANES]
    wide[pl.ds(2 * first + 1, n, stride=2), :] = block[:, LANES:]


def merged(wide, first, n):
    left = wide[pl.ds(2 * first, n, stride=2), :]
    right = wide[pl.ds(2 * first + 1, n, stride=2), :]
    return jnp.concatenate([left, right], axis=1)


def coag_kernel(blocks, cls_ref, dust_ref, ker_ref, ids_ref, coag_ref, out_ref, wide, picked, cls_wide, scaled, *rest):
    ids, sem = rest[:4], rest[4]
    step = pl.program_id(0)
    rows = dust_ref.shape[0]
    copies = [pltpu.make_async_copy(scaled.at[pl.ds(k, 1), :], ids[k], sem.at[k]) for k in range(4)]

    @pl.when(step == 0)
    def _():
        scaled[...] = ids_ref[...] * 2
        for copy in copies:
            copy.start()

    for k in range(rows // LANES):
        cls_wide[k * LANES:(k + 1) * LANES, :] = column(cls_ref[k:k + 1, :])
    group = cls_wide[...]
    pair = (group >> 1).astype(i16)
    odd = (group & 1) == 1
    masks = [pair == p for p in range(4)]
    block = dust_ref[...].astype(f32)
    state = [block[:, :LANES], block[:, LANES:]]
    for substep in range(SUBSTEPS):
        following = []
        for s in range(2):
            operand = state[s].astype(bf16)
            zero = jnp.zeros_like(operand)
            spread = jnp.concatenate([jnp.where(m, operand, zero) for m in masks], axis=1)
            weights = jnp.concatenate(
                [jnp.concatenate([ker_ref[2 * p, s], ker_ref[2 * p + 1, s]], axis=1) for p in range(4)], axis=0
            )
            both = jnp.dot(spread, weights, preferred_element_type=f32)
            product = jnp.where(odd, both[:, LANES:], both[:, :LANES])
            mean_square = jnp.mean(state[s] * state[s], axis=1, keepdims=True)
            following.append(state[s] + product * (mean_square / (1.0 + mean_square)))
        state = following
    rounded = jnp.concatenate(state, axis=1).astype(bf16)
    coag_ref[...] = rounded
    interleave(wide, step * rows, rounded.astype(f32))

    @pl.when(step == blocks - 1)
    def _():
        for copy in copies:
            copy.wait()

        def pick(i, carry):
            for v in range(8):
                at = i * 8 + v
                for k in range(4):
                    row = pl.multiple_of(ids[k][0, at], 2)
                    picked[pl.ds(pl.multiple_of(2 * (k * CHUNK) + 2 * at, 2), 2), :] = wide[pl.ds(row, 2), :]
            return carry

        lax.fori_loop(0, CHUNK // 8, pick, 0)

        def narrow(i, carry):
            first = pl.multiple_of(i * 256, 256)
            out_ref[pl.ds(first, 256), :] = merged(picked, first, 256).astype(bf16)
            return carry

        lax.fori_loop(0, 4 * CHUNK // 256, narrow, 0)


def coagulate(dust, classes, kernels, export_ids):
    rows = dust.shape[0]
    block = 1024
    blocks = rows // block
    return pl.pallas_call(
        functools.partial(coag_kernel, blocks),
        grid=(blocks,),
        in_specs=[
            pl.BlockSpec((block // LANES, LANES), lambda i: (i, 0)),
            pl.BlockSpec((block, 256), lambda i: (i, 0)),
            pl.BlockSpec(kernels.shape, lambda i: (0, 0, 0, 0)),
            pl.BlockSpec(export_ids.shape, lambda i: (0, 0)),
        ],
        out_specs=[
            pl.BlockSpec((block, 256), lambda i: (i, 0)),
            pl.BlockSpec((4 * CHUNK, 256), lambda i: (0, 0)),
        ],
        out_shape=[
            jax.ShapeDtypeStruct((rows, 256), bf16),
            jax.ShapeDtypeStruct((4 * CHUNK, 256), bf16),
        ],
        scratch_shapes=[
            pltpu.VMEM((2 * rows, LANES), f32),
            pltpu.VMEM((8 * CHUNK, LANES), f32),
            pltpu.VMEM((block, LANES), i32),
            pltpu.VMEM(export_ids.shape, i32),
            *[pltpu.SMEM((1, CHUNK), i32)] * 4,
            pltpu.SemaphoreType.DMA((4,)),
        ],
        compiler_params=pltpu.CompilerParams(vmem_limit_bytes=56 << 20),
        name="coagulate",
    )(classes.reshape(rows // LANES, LANES), dust, kernels, export_ids)


FACES = 6
CAP = 16
UNROLL = 32


def step_kernel(n_dx, n_dy, outbound_ref, coag_ref, coef_ref, faces_ref, mig_ref, count_ref, next_ref, arrive_ref,
                ext, coefs, wide, picked, ghosts, leave, updated, scaled, *rest):
    ids = rest[:FACES]
    send_sem, recv_sem, ids_sem, own_sem, out_sem, leave_sem, arrive_sem = rest[FACES:]
    rows = coag_ref.shape[0]
    count = n_dx * n_dy
    a, b = lax.axis_index("dx"), lax.axis_index("dy")
    me = a * n_dy + b

    def position(device):
        return (device // n_dy, lax.rem(device, n_dy))

    def greet(k, carry):
        pl.semaphore_signal(
            pltpu.get_barrier_semaphore(), inc=1, device_id=position(lax.rem(me + k, count)), device_id_type=MESH)
        return carry

    lax.fori_loop(1, count, greet, 0)
    scaled[...] = faces_ref[...] * 2
    lookups = [pltpu.make_async_copy(scaled.at[pl.ds(f, 1), :], ids[f], ids_sem.at[f]) for f in range(FACES)]
    for copy in lookups:
        copy.start()
    pl.semaphore_wait(pltpu.get_barrier_semaphore(), count - 1)

    peers = [
        (lax.rem(a + 1, n_dx), b),
        (lax.rem(a + n_dx - 1, n_dx), b),
        (a, lax.rem(b + 1, n_dy)),
        (a, lax.rem(b + n_dy - 1, n_dy)),
    ]
    halo = {}
    for k in (2, 3, 0, 1):
        halo[k] = pltpu.make_async_remote_copy(
            src_ref=outbound_ref.at[pl.ds(k * CHUNK, CHUNK)],
            dst_ref=ghosts.at[pl.ds(k * CHUNK, CHUNK)],
            send_sem=send_sem.at[k],
            recv_sem=recv_sem.at[k],
            device_id=peers[k],
            device_id_type=MESH,
        )
        halo[k].start()

    def spread(i, carry):
        first = pl.multiple_of(i * LANES, LANES)
        block = coef_ref[:, pl.ds(first, LANES)]
        kept = 1.0 - jnp.sum(block, axis=0, keepdims=True)
        for f in range(FACES + 1):
            coefs[pl.ds(f * rows + first, LANES), :] = column(block[f:f + 1, :] if f < FACES else kept)
        interleave(ext, first, coag_ref[pl.ds(first, LANES), :].astype(f32))
        return carry

    lax.fori_loop(0, rows // LANES, spread, 0)
    for copy in lookups:
        copy.wait()
    for k in (0, 1, 2, 3):
        halo[k].wait()

        def widen(i, carry):
            first = pl.multiple_of(i * LANES, LANES)
            interleave(ext, rows + k * CHUNK + first, ghosts[pl.ds(k * CHUNK + first, LANES), :].astype(f32))
            return carry

        lax.fori_loop(0, CHUNK // LANES, widen, 0)

    def weighted(row, cell, f):
        return ext[pl.ds(row, 2), :] * coefs[pl.ds(f * rows + cell, 2, stride=0), :]

    def stay(i, carry):
        first = pl.multiple_of(i * UNROLL, UNROLL)
        for j in range(UNROLL):
            cell = first + j
            total = weighted(2 * cell, cell, FACES)
            for f in range(FACES):
                total = total + weighted(ids[f][0, cell], cell, f)
            wide[pl.ds(pl.multiple_of(2 * cell, 2), 2), :] = total
        updated[pl.ds(first, UNROLL), :] = merged(wide, first, UNROLL).astype(bf16)
        return carry

    lax.fori_loop(0, rows // UNROLL, stay, 0)
    out = pltpu.make_async_copy(updated, next_ref, out_sem)
    out.start()

    def place(domain):
        return pl.ds(pl.multiple_of(domain * CAP, CAP), CAP)

    slot = lax.broadcasted_iota(i32, (CAP, 256), 0)

    def pack(domain):
        for j in range(CAP):
            picked[pl.ds(2 * j, 2), :] = wide[pl.ds(2 * mig_ref[j, domain], 2), :]
        kept = jnp.clip(count_ref[0, domain] - slot, 0, 1).astype(f32)
        leave[place(domain), :] = (merged(picked, 0, CAP) * kept).astype(bf16)

    def send(k, carry):
        domain = lax.rem(me + k, count)
        pack(domain)
        pltpu.make_async_remote_copy(
            src_ref=leave.at[place(domain)],
            dst_ref=arrive_ref.at[place(me)],
            send_sem=leave_sem,
            recv_sem=arrive_sem,
            device_id=position(domain),
            device_id_type=MESH,
        ).start()
        return carry

    lax.fori_loop(1, count, send, 0)
    pack(me)
    own = pltpu.make_async_copy(leave.at[place(me)], arrive_ref.at[place(me)], own_sem)
    own.start()
    own.wait()
    others = pl.ds(0, (count - 1) * CAP)
    pltpu.make_async_copy(leave.at[others], leave.at[others], leave_sem).wait()
    pltpu.make_async_copy(arrive_ref.at[others], arrive_ref.at[others], arrive_sem).wait()
    out.wait()


def advance(outbound, coag, face_coef, faces, mig_ids, counts, n_dx, n_dy):
    rows = coag.shape[0]
    vmem = pl.BlockSpec(memory_space=pltpu.VMEM)
    smem = pl.BlockSpec(memory_space=pltpu.SMEM)
    hbm = pl.BlockSpec(memory_space=pl.ANY)
    moved = mig_ids.shape[0] * mig_ids.shape[1]
    dma = pltpu.SemaphoreType.DMA
    return pl.pallas_call(
        functools.partial(step_kernel, n_dx, n_dy),
        in_specs=[hbm, vmem, vmem, vmem, smem, smem],
        out_specs=[hbm, hbm],
        out_shape=[jax.ShapeDtypeStruct((rows, 256), bf16), jax.ShapeDtypeStruct((moved, 256), bf16)],
        scratch_shapes=[
            pltpu.VMEM((2 * rows + 2 * 4 * CHUNK, LANES), f32),
            pltpu.VMEM(((FACES + 1) * rows, LANES), f32),
            pltpu.VMEM((2 * rows, LANES), f32),
            pltpu.VMEM((2 * CAP, LANES), f32),
            pltpu.VMEM((4 * CHUNK, 256), bf16),
            pltpu.VMEM((moved, 256), bf16),
            pltpu.VMEM((rows, 256), bf16),
            pltpu.VMEM((FACES, rows), i32),
            *[pltpu.SMEM((1, rows), i32)] * FACES,
            dma((4,)), dma((4,)), dma((FACES,)), dma, dma, dma, dma,
        ],
        compiler_params=pltpu.CompilerParams(
            vmem_limit_bytes=56 << 20, collective_id=0, has_side_effects=True),
        name="advance",
    )(outbound, coag, face_coef, faces, mig_ids, counts)


def body(n_dx, n_dy, dust, classes, kernels, export_ids, faces, face_coef, mig_ids, mig_counts):
    coag, outbound = coagulate(dust, classes, kernels, export_ids[0])
    return advance(outbound, coag, face_coef, faces, mig_ids.T, mig_counts, n_dx, n_dy)


def solution(mesh):
    return jax.shard_map(
        functools.partial(body, mesh.shape["dx"], mesh.shape["dy"]),
        mesh=mesh,
        in_specs=(
            P(("dx", "dy"), None),
            P(("dx", "dy")),
            P(),
            P(("dx", "dy"), None, None),
            P(None, ("dx", "dy")),
            P(None, ("dx", "dy")),
            P(("dx", "dy"), None),
            P(("dx", "dy"), None),
        ),
        out_specs=(P(("dx", "dy"), None), P(("dx", "dy"), None)),
        check_vma=False,
    )
```

```python
import functools
import jax
import jax.numpy as jnp
from jax import lax
from jax.experimental import pallas as pl
from jax.experimental.pallas import tpu as pltpu
from jax.sharding import PartitionSpec as P

SUBSTEPS = 6
SPECIES = 2
LANES = 128
FACES = 6
BLOCK = 1024
UNROLL = 32
MESH = pl.DeviceIdType.MESH
f32, bf16, i32, i16 = jnp.float32, jnp.bfloat16, jnp.int32, jnp.int16


def column(row):
    return jnp.broadcast_to(row, (LANES, LANES)).T


def merged(wide, first, n):
    return jnp.concatenate([wide[pl.ds(2 * first + s, n, stride=2), :] for s in range(SPECIES)], axis=1)


def step_kernel(n_dx, n_dy, dust_ref, cls_ref, ker_ref, export_ref, coef_ref, faces_ref, mig_ref, count_ref,
                next_ref, arrive_ref, ext, coefs, wide, picked, outbound, ghosts, leave, updated,
                scaled_faces, scaled_exports, cls_wide, *rest):
    ids, exports = rest[:FACES], rest[FACES:FACES + 4]
    send_sem, recv_sem, ids_sem, own_sem, out_sem, leave_sem, arrive_sem = rest[FACES + 4:]
    rows = dust_ref.shape[0]
    exported = export_ref.shape[1]
    cap = mig_ref.shape[0]
    count = n_dx * n_dy
    a, b = lax.axis_index("dx"), lax.axis_index("dy")
    me = a * n_dy + b

    def position(device):
        return (device // n_dy, lax.rem(device, n_dy))

    def greet(k, carry):
        pl.semaphore_signal(
            pltpu.get_barrier_semaphore(), inc=1, device_id=position(lax.rem(me + k, count)), device_id_type=MESH)
        return carry

    lax.fori_loop(1, count, greet, 0)

    scaled_exports[...] = export_ref[...] * 2
    scaled_faces[...] = faces_ref[...] * 2
    lookups = [
        pltpu.make_async_copy(scaled_exports.at[pl.ds(k, 1), :], exports[k], ids_sem.at[FACES + k]) for k in range(4)
    ] + [
        pltpu.make_async_copy(scaled_faces.at[pl.ds(f, 1), :], ids[f], ids_sem.at[f]) for f in range(FACES)
    ]
    for copy in lookups:
        copy.start()
    for k in range(rows // LANES):
        cls_wide[k * LANES:(k + 1) * LANES, :] = column(cls_ref[k:k + 1, :])

    def substeps(s):
        weights = [
            jnp.concatenate([ker_ref[2 * p, s], ker_ref[2 * p + 1, s]], axis=1) for p in range(ker_ref.shape[0] // 2)
        ]

        def run(i, carry):
            firsts = [pl.multiple_of((2 * i + h) * BLOCK, BLOCK) for h in range(2)]
            groups = [cls_wide[pl.ds(first, BLOCK), :] for first in firsts]
            odd = [(group & 1) == 1 for group in groups]
            pairs = [(group >> 1).astype(i16) for group in groups]
            state = [dust_ref[pl.ds(first, BLOCK), s * LANES:(s + 1) * LANES].astype(f32) for first in firsts]
            for substep in range(SUBSTEPS):
                for h in range(2):
                    operand = state[h].astype(bf16)
                    zero = jnp.zeros_like(operand)
                    spread = jnp.concatenate(
                        [jnp.where(pairs[h] == p, operand, zero) for p in range(len(weights))], axis=1)
                    both = jnp.dot(spread, jnp.concatenate(weights, axis=0), preferred_element_type=f32)
                    product = jnp.where(odd[h], both[:, LANES:], both[:, :LANES])
                    mean_square = jnp.mean(state[h] * state[h], axis=1, keepdims=True)
                    state[h] = state[h] + product * (mean_square / (1.0 + mean_square))
            for h in range(2):
                ext[pl.ds(2 * firsts[h] + s, BLOCK, stride=2), :] = state[h].astype(bf16).astype(f32)
            return carry

        lax.fori_loop(0, rows // (2 * BLOCK), run, 0)

    peers = [
        (lax.rem(a + 1, n_dx), b),
        (lax.rem(a + n_dx - 1, n_dx), b),
        (a, lax.rem(b + 1, n_dy)),
        (a, lax.rem(b + n_dy - 1, n_dy)),
    ]

    def halo(s, k):
        place = pl.ds(k * exported, exported)
        return pltpu.make_async_remote_copy(
            src_ref=outbound.at[s, place],
            dst_ref=ghosts.at[s, place],
            send_sem=send_sem.at[s * 4 + k],
            recv_sem=recv_sem.at[s * 4 + k],
            device_id=peers[k],
            device_id_type=MESH,
        )

    for s in range(SPECIES):
        substeps(s)
        if s == 0:
            for copy in lookups:
                copy.wait()
            pl.semaphore_wait(pltpu.get_barrier_semaphore(), count - 1)
        for k in (2, 3, 0, 1):

            def pick(i, carry):
                first = pl.multiple_of(i * UNROLL, UNROLL)
                for j in range(UNROLL):
                    picked[pl.ds(j, 1), :] = ext[pl.ds(exports[k][0, first + j] + s, 1), :]
                outbound[s, pl.ds(k * exported + first, UNROLL), :] = picked[...].astype(bf16)
                return carry

            lax.fori_loop(0, exported // UNROLL, pick, 0)
            halo(s, k).start()

    def spread(i, carry):
        first = pl.multiple_of(i * LANES, LANES)
        block = coef_ref[:, pl.ds(first, LANES)]
        kept = 1.0 - jnp.sum(block, axis=0, keepdims=True)
        for f in range(FACES + 1):
            coefs[pl.ds(f * rows + first, LANES), :] = column(block[f:f + 1, :] if f < FACES else kept)
        return carry

    lax.fori_loop(0, rows // LANES, spread, 0)
    for s in range(SPECIES):
        for k in (0, 1, 2, 3):
            halo(s, k).wait()

            def widen(i, carry):
                first = pl.multiple_of(i * LANES, LANES)
                at = rows + k * exported + first
                ext[pl.ds(2 * at + s, LANES, stride=2), :] = ghosts[
                    s, pl.ds(k * exported + first, LANES), :].astype(f32)
                return carry

            lax.fori_loop(0, exported // LANES, widen, 0)

    def weighted(row, cell, f):
        return ext[pl.ds(row, 2), :] * coefs[pl.ds(f * rows + cell, 2, stride=0), :]

    def stay(i, carry):
        first = pl.multiple_of(i * UNROLL, UNROLL)
        for j in range(UNROLL):
            cell = first + j
            total = weighted(2 * cell, cell, FACES)
            for f in range(FACES):
                total = total + weighted(ids[f][0, cell], cell, f)
            wide[pl.ds(2 * cell, 2), :] = total
        updated[pl.ds(first, UNROLL), :] = merged(wide, first, UNROLL).astype(bf16)
        return carry

    lax.fori_loop(0, rows // UNROLL, stay, 0)
    out = pltpu.make_async_copy(updated, next_ref, out_sem)
    out.start()

    def place(domain):
        return pl.ds(pl.multiple_of(domain * cap, cap), cap)

    slot = lax.broadcasted_iota(i32, (cap, SPECIES * LANES), 0)

    def pack(domain):
        for j in range(cap):
            picked[pl.ds(2 * j, 2), :] = wide[pl.ds(2 * mig_ref[j, domain], 2), :]
        kept = jnp.clip(count_ref[0, domain] - slot, 0, 1).astype(f32)
        leave[place(domain), :] = (merged(picked, 0, cap) * kept).astype(bf16)

    def send(k, carry):
        domain = lax.rem(me + k, count)
        pack(domain)
        pltpu.make_async_remote_copy(
            src_ref=leave.at[place(domain)],
            dst_ref=arrive_ref.at[place(me)],
            send_sem=leave_sem,
            recv_sem=arrive_sem,
            device_id=position(domain),
            device_id_type=MESH,
        ).start()
        return carry

    lax.fori_loop(1, count, send, 0)
    pack(me)
    own = pltpu.make_async_copy(leave.at[place(me)], arrive_ref.at[place(me)], own_sem)
    own.start()
    own.wait()
    others = pl.ds(0, (count - 1) * cap)
    pltpu.make_async_copy(leave.at[others], leave.at[others], leave_sem).wait()
    pltpu.make_async_copy(arrive_ref.at[others], arrive_ref.at[others], arrive_sem).wait()
    out.wait()


def advance(dust, classes, kernels, export_ids, face_coef, faces, mig_ids, counts, n_dx, n_dy):
    rows, width = dust.shape
    sent = export_ids.shape[0] * export_ids.shape[1]
    moved = mig_ids.shape[0] * mig_ids.shape[1]
    vmem = pl.BlockSpec(memory_space=pltpu.VMEM)
    smem = pl.BlockSpec(memory_space=pltpu.SMEM)
    hbm = pl.BlockSpec(memory_space=pl.ANY)
    dma = pltpu.SemaphoreType.DMA
    return pl.pallas_call(
        functools.partial(step_kernel, n_dx, n_dy),
        in_specs=[vmem] * 6 + [smem, smem],
        out_specs=[hbm, hbm],
        out_shape=[jax.ShapeDtypeStruct((rows, width), bf16), jax.ShapeDtypeStruct((moved, width), bf16)],
        scratch_shapes=[
            pltpu.VMEM((2 * (rows + sent), LANES), f32),
            pltpu.VMEM(((FACES + 1) * rows, LANES), f32),
            pltpu.VMEM((2 * rows, LANES), f32),
            pltpu.VMEM((UNROLL, LANES), f32),
            pltpu.VMEM((SPECIES, sent, LANES), bf16),
            pltpu.VMEM((SPECIES, sent, LANES), bf16),
            pltpu.VMEM((moved, width), bf16),
            pltpu.VMEM((rows, width), bf16),
            pltpu.VMEM(faces.shape, i32),
            pltpu.VMEM(export_ids.shape, i32),
            pltpu.VMEM((rows, LANES), i32),
            *[pltpu.SMEM((1, rows), i32)] * FACES,
            *[pltpu.SMEM((1, export_ids.shape[1]), i32)] * 4,
            dma((8,)), dma((8,)), dma((FACES + 4,)), dma, dma, dma, dma,
        ],
        compiler_params=pltpu.CompilerParams(
            vmem_limit_bytes=60 << 20, collective_id=0, has_side_effects=True),
        name="advance",
    )(dust, classes, kernels, export_ids, face_coef, faces, mig_ids, counts)


def hand_over_kernel(pieces, *refs):
    sources, targets, buffers, in_sem, out_sem = refs[:2], refs[2:4], refs[4:6], refs[6], refs[7]
    loads, stores = [], []
    for n in range(2):
        rows = sources[n].shape[0] // pieces
        for k in range(pieces):
            part = pl.ds(k * rows, rows)
            loads.append(pltpu.make_async_copy(sources[n].at[part], buffers[n].at[part], in_sem.at[n * pieces + k]))
            stores.append(pltpu.make_async_copy(buffers[n].at[part], targets[n].at[part], out_sem.at[n * pieces + k]))
    for load in loads:
        load.start()
    for load, store in zip(loads, stores):
        load.wait()
        store.start()
    for store in stores:
        store.wait()


def hand_over(*arrays):
    hbm = pl.BlockSpec(memory_space=pl.ANY)
    pieces = 4
    return pl.pallas_call(
        functools.partial(hand_over_kernel, pieces),
        in_specs=[hbm] * 2,
        out_specs=[hbm] * 2,
        out_shape=[jax.ShapeDtypeStruct(x.shape, x.dtype) for x in arrays],
        scratch_shapes=[
            *[pltpu.VMEM(x.shape, x.dtype) for x in arrays],
            pltpu.SemaphoreType.DMA((2 * pieces,)),
            pltpu.SemaphoreType.DMA((2 * pieces,)),
        ],
        name="hand_over",
    )(*arrays)


def body(n_dx, n_dy, dust, classes, kernels, export_ids, faces, face_coef, mig_ids, mig_counts):
    updated, arrivals = advance(
        dust, classes.reshape(-1, LANES), kernels, export_ids[0], face_coef, faces, mig_ids.T, mig_counts, n_dx, n_dy)
    return tuple(hand_over(updated, arrivals))


def solution(mesh):
    return jax.shard_map(
        functools.partial(body, mesh.shape["dx"], mesh.shape["dy"]),
        mesh=mesh,
        in_specs=(
            P(("dx", "dy"), None),
            P(("dx", "dy")),
            P(),
            P(("dx", "dy"), None, None),
            P(None, ("dx", "dy")),
            P(None, ("dx", "dy")),
            P(("dx", "dy"), None),
            P(("dx", "dy"), None),
        ),
        out_specs=(P(("dx", "dy"), None), P(("dx", "dy"), None)),
        check_vma=False,
    )
```

```python
import functools
import jax
import jax.numpy as jnp
from jax import lax
from jax.experimental import pallas as pl
from jax.experimental.pallas import tpu as pltpu
from jax.sharding import PartitionSpec as P

SUBSTEPS = 6
SPECIES = 2
LANES = 128
FACES = 6
BLOCK = 1024
PARTS = 4
UNROLL = 16
PICKS = 8
PICK_UNROLL = 4
MESH = pl.DeviceIdType.MESH
f32, bf16, i32, i16 = jnp.float32, jnp.bfloat16, jnp.int32, jnp.int16


def column(row):
    return jnp.broadcast_to(row, (LANES, LANES)).T


def merged(wide, first, n):
    return jnp.concatenate([wide[pl.ds(2 * first + s, n, stride=2), :] for s in range(SPECIES)], axis=1)


def step_kernel(n_dx, n_dy, dust_ref, cls_ref, ker_ref, export_ref, coef_ref, faces_ref, mig_ref, count_ref,
                next_ref, arrive_ref, dust, kernels, ext, coefs, wide, picked, outbound, ghosts, leave, updated,
                scaled_faces, scaled_exports, cls_wide, *rest):
    ids, exports = rest[:FACES * PARTS], rest[FACES * PARTS:FACES * PARTS + 4 * PICKS]
    load_sem, send_sem, recv_sem, ids_sem, own_sem, out_sem, leave_sem, arrive_sem = rest[FACES * PARTS + 4 * PICKS:]
    rows = dust_ref.shape[0]
    exported = export_ref.shape[1]
    cap = mig_ref.shape[0]
    count = n_dx * n_dy
    part_rows, pick_rows = rows // PARTS, exported // PICKS
    a, b = lax.axis_index("dx"), lax.axis_index("dy")
    me = a * n_dy + b

    def position(device):
        return (device // n_dy, lax.rem(device, n_dy))

    loads = [pltpu.make_async_copy(ker_ref, kernels, load_sem.at[0])]
    for n in range(rows // (2 * BLOCK)):
        part = pl.ds(n * 2 * BLOCK, 2 * BLOCK)
        loads.append(pltpu.make_async_copy(dust_ref.at[part], dust.at[part], load_sem.at[1 + n]))
    for copy in loads:
        copy.start()

    def greet(k):
        pl.semaphore_signal(
            pltpu.get_barrier_semaphore(), inc=1, device_id=position(lax.rem(me + k, count)), device_id_type=MESH)

    def greet_eight(i, carry):
        for j in range(8):
            greet(8 * i + j)
        return carry

    for k in range(1, 8):
        greet(k)
    lax.fori_loop(1, count // 8, greet_eight, 0)

    scaled_exports[...] = export_ref[...] * 2
    scaled_faces[...] = faces_ref[...] * 2
    lookups = []
    for k in range(4):
        for u in range(PICKS):
            n = k * PICKS + u
            lookups.append(pltpu.make_async_copy(
                scaled_exports.at[pl.ds(k, 1), pl.ds(u * pick_rows, pick_rows)], exports[n], ids_sem.at[n]))
    for f in range(FACES):
        for u in range(PARTS):
            n = f * PARTS + u
            lookups.append(pltpu.make_async_copy(
                scaled_faces.at[pl.ds(f, 1), pl.ds(u * part_rows, part_rows)], ids[n], ids_sem.at[4 * PICKS + n]))
    for copy in lookups:
        copy.start()
    for k in range(rows // LANES):
        cls_wide[k * LANES:(k + 1) * LANES, :] = column(cls_ref[k:k + 1, :])

    def substeps(s):
        weights = [
            jnp.concatenate([kernels[2 * p, s], kernels[2 * p + 1, s]], axis=1) for p in range(kernels.shape[0] // 2)
        ]

        def run(i, carry):
            firsts = [pl.multiple_of((2 * i + h) * BLOCK, BLOCK) for h in range(2)]
            groups = [cls_wide[pl.ds(first, BLOCK), :] for first in firsts]
            odd = [(group & 1) == 1 for group in groups]
            pairs = [(group >> 1).astype(i16) for group in groups]
            state = [dust[pl.ds(first, BLOCK), s * LANES:(s + 1) * LANES].astype(f32) for first in firsts]
            for substep in range(SUBSTEPS):
                for h in range(2):
                    operand = state[h].astype(bf16)
                    zero = jnp.zeros_like(operand)
                    spread = jnp.concatenate(
                        [jnp.where(pairs[h] == p, operand, zero) for p in range(len(weights))], axis=1)
                    both = jnp.dot(spread, jnp.concatenate(weights, axis=0), preferred_element_type=f32)
                    product = jnp.where(odd[h], both[:, LANES:], both[:, :LANES])
                    squares = jnp.sum(state[h] * state[h], axis=1, keepdims=True)
                    state[h] = state[h] + product * (squares / (LANES + squares))
            for h in range(2):
                ext[pl.ds(2 * firsts[h] + s, BLOCK, stride=2), :] = state[h].astype(bf16).astype(f32)
            return carry

        lax.fori_loop(0, rows // (2 * BLOCK), run, 0)

    peers = [
        (lax.rem(a + 1, n_dx), b),
        (lax.rem(a + n_dx - 1, n_dx), b),
        (a, lax.rem(b + 1, n_dy)),
        (a, lax.rem(b + n_dy - 1, n_dy)),
    ]

    def halo(s, k):
        place = pl.ds(k * exported, exported)
        return pltpu.make_async_remote_copy(
            src_ref=outbound.at[s, place],
            dst_ref=ghosts.at[s, place],
            send_sem=send_sem.at[s * 4 + k],
            recv_sem=recv_sem.at[s * 4 + k],
            device_id=peers[k],
            device_id_type=MESH,
        )

    for copy in loads:
        copy.wait()
    for s in range(SPECIES):
        substeps(s)
        if s == 0:
            for copy in lookups:
                copy.wait()
            pl.semaphore_wait(pltpu.get_barrier_semaphore(), count - 1)
        for k in (2, 3, 0, 1):

            def pick(i, carry):
                for v in range(PICK_UNROLL):
                    at = i * PICK_UNROLL + v
                    for u in range(PICKS):
                        row = exports[k * PICKS + u][0, at] + s
                        picked[pl.ds(u * pick_rows + at, 1), :] = ext[pl.ds(row, 1), :]
                return carry

            lax.fori_loop(0, pick_rows // PICK_UNROLL, pick, 0)

            def narrow(i, carry):
                first = pl.multiple_of(i * 256, 256)
                outbound[s, pl.ds(k * exported + first, 256), :] = picked[pl.ds(first, 256), :].astype(bf16)
                return carry

            lax.fori_loop(0, exported // 256, narrow, 0)
            halo(s, k).start()

    def spread(i, carry):
        first = pl.multiple_of(i * LANES, LANES)
        for f in range(FACES):
            weight = column(coef_ref[f:f + 1, pl.ds(first, LANES)])
            for half in range(2):
                coefs[pl.ds(2 * (f * rows + first) + half, LANES, stride=2), :] = weight
        return carry

    lax.fori_loop(0, rows // LANES, spread, 0)
    for s in range(SPECIES):
        for k in (0, 1, 2, 3):
            halo(s, k).wait()

            def widen(i, carry):
                first = pl.multiple_of(i * LANES, LANES)
                at = rows + k * exported + first
                ext[pl.ds(2 * at + s, LANES, stride=2), :] = ghosts[
                    s, pl.ds(k * exported + first, LANES), :].astype(f32)
                return carry

            lax.fori_loop(0, exported // LANES, widen, 0)

    def stay(i, carry):
        at = pl.multiple_of(i * UNROLL, UNROLL)
        for u in range(PARTS):
            first = pl.multiple_of(u * part_rows + at, UNROLL)
            for j in range(UNROLL):
                pair = 2 * (first + j)
                own = ext[pl.ds(pair, 2), :]
                total = own
                for f in range(FACES):
                    row = ids[f * PARTS + u][0, at + j]
                    total = total + coefs[pl.ds(2 * f * rows + pair, 2), :] * (ext[pl.ds(row, 2), :] - own)
                wide[pl.ds(pair, 2), :] = total
            updated[pl.ds(first, UNROLL), :] = merged(wide, first, UNROLL).astype(bf16)
        return carry

    lax.fori_loop(0, part_rows // UNROLL, stay, 0)
    out = pltpu.make_async_copy(updated, next_ref, out_sem)
    out.start()

    def place(domain):
        return pl.ds(pl.multiple_of(domain * cap, cap), cap)

    slot = lax.broadcasted_iota(i32, (cap, SPECIES * LANES), 0)

    def pack(domain):
        for j in range(cap):
            picked[pl.ds(2 * j, 2), :] = wide[pl.ds(2 * mig_ref[j, domain], 2), :]
        kept = jnp.clip(count_ref[0, domain] - slot, 0, 1).astype(f32)
        leave[place(domain), :] = (merged(picked, 0, cap) * kept).astype(bf16)

    def send(k, carry):
        domain = lax.rem(me + k, count)
        pack(domain)
        pltpu.make_async_remote_copy(
            src_ref=leave.at[place(domain)],
            dst_ref=arrive_ref.at[place(me)],
            send_sem=leave_sem,
            recv_sem=arrive_sem,
            device_id=position(domain),
            device_id_type=MESH,
        ).start()
        return carry

    lax.fori_loop(1, count, send, 0)
    pack(me)
    own = pltpu.make_async_copy(leave.at[place(me)], arrive_ref.at[place(me)], own_sem)
    own.start()
    own.wait()
    others = pl.ds(0, (count - 1) * cap)
    pltpu.make_async_copy(leave.at[others], leave.at[others], leave_sem).wait()
    pltpu.make_async_copy(arrive_ref.at[others], arrive_ref.at[others], arrive_sem).wait()
    out.wait()


def advance(dust, classes, kernels, export_ids, face_coef, faces, mig_ids, counts, n_dx, n_dy):
    rows, width = dust.shape
    sent = export_ids.shape[0] * export_ids.shape[1]
    moved = mig_ids.shape[0] * mig_ids.shape[1]
    vmem = pl.BlockSpec(memory_space=pltpu.VMEM)
    smem = pl.BlockSpec(memory_space=pltpu.SMEM)
    hbm = pl.BlockSpec(memory_space=pl.ANY)
    dma = pltpu.SemaphoreType.DMA
    return pl.pallas_call(
        functools.partial(step_kernel, n_dx, n_dy),
        in_specs=[hbm, vmem, hbm, vmem, vmem, vmem, smem, smem],
        out_specs=[hbm, hbm],
        out_shape=[jax.ShapeDtypeStruct((rows, width), bf16), jax.ShapeDtypeStruct((moved, width), bf16)],
        scratch_shapes=[
            pltpu.VMEM(dust.shape, bf16),
            pltpu.VMEM(kernels.shape, bf16),
            pltpu.VMEM((2 * (rows + sent), LANES), f32),
            pltpu.VMEM((2 * FACES * rows, LANES), f32),
            pltpu.VMEM((2 * rows, LANES), f32),
            pltpu.VMEM((export_ids.shape[1], LANES), f32),
            pltpu.VMEM((SPECIES, sent, LANES), bf16),
            pltpu.VMEM((SPECIES, sent, LANES), bf16),
            pltpu.VMEM((moved, width), bf16),
            pltpu.VMEM((rows, width), bf16),
            pltpu.VMEM(faces.shape, i32),
            pltpu.VMEM(export_ids.shape, i32),
            pltpu.VMEM((rows, LANES), i32),
            *[pltpu.SMEM((1, rows // PARTS), i32)] * (FACES * PARTS),
            *[pltpu.SMEM((1, export_ids.shape[1] // PICKS), i32)] * (4 * PICKS),
            dma((1 + rows // (2 * BLOCK),)), dma((8,)), dma((8,)), dma((FACES * PARTS + 4 * PICKS,)),
            dma, dma, dma, dma,
        ],
        compiler_params=pltpu.CompilerParams(
            vmem_limit_bytes=60 << 20, collective_id=0, has_side_effects=True),
        name="advance",
    )(dust, classes, kernels, export_ids, face_coef, faces, mig_ids, counts)


def hand_over_kernel(pieces, *refs):
    sources, targets, buffers, in_sem, out_sem = refs[:2], refs[2:4], refs[4:6], refs[6], refs[7]
    loads, stores = [], []
    for n in range(2):
        rows = sources[n].shape[0] // pieces
        for k in range(pieces):
            part = pl.ds(k * rows, rows)
            loads.append(pltpu.make_async_copy(sources[n].at[part], buffers[n].at[part], in_sem.at[n * pieces + k]))
            stores.append(pltpu.make_async_copy(buffers[n].at[part], targets[n].at[part], out_sem.at[n * pieces + k]))
    for load in loads:
        load.start()
    for load, store in zip(loads, stores):
        load.wait()
        store.start()
    for store in stores:
        store.wait()


def hand_over(*arrays):
    hbm = pl.BlockSpec(memory_space=pl.ANY)
    pieces = 4
    return pl.pallas_call(
        functools.partial(hand_over_kernel, pieces),
        in_specs=[hbm] * 2,
        out_specs=[hbm] * 2,
        out_shape=[jax.ShapeDtypeStruct(x.shape, x.dtype) for x in arrays],
        scratch_shapes=[
            *[pltpu.VMEM(x.shape, x.dtype) for x in arrays],
            pltpu.SemaphoreType.DMA((2 * pieces,)),
            pltpu.SemaphoreType.DMA((2 * pieces,)),
        ],
        name="hand_over",
    )(*arrays)


def body(n_dx, n_dy, dust, classes, kernels, export_ids, faces, face_coef, mig_ids, mig_counts):
    updated, arrivals = advance(
        dust, classes.reshape(-1, LANES), kernels, export_ids[0], face_coef, faces, mig_ids.T, mig_counts, n_dx, n_dy)
    return tuple(hand_over(updated, arrivals))


def solution(mesh):
    return jax.shard_map(
        functools.partial(body, mesh.shape["dx"], mesh.shape["dy"]),
        mesh=mesh,
        in_specs=(
            P(("dx", "dy"), None),
            P(("dx", "dy")),
            P(),
            P(("dx", "dy"), None, None),
            P(None, ("dx", "dy")),
            P(None, ("dx", "dy")),
            P(("dx", "dy"), None),
            P(("dx", "dy"), None),
        ),
        out_specs=(P(("dx", "dy"), None), P(("dx", "dy"), None)),
        check_vma=False,
    )
```

```python
import functools
import jax
import jax.numpy as jnp
from jax import lax
from jax.experimental import pallas as pl
from jax.experimental.pallas import tpu as pltpu
from jax.sharding import PartitionSpec as P

SUBSTEPS = 6
SPECIES = 2
LANES = 128
FACES = 6
BLOCK = 1024
PARTS = 1
UNROLL = 32
PICKS = 8
PICK_UNROLL = 4
MESH = pl.DeviceIdType.MESH
f32, bf16, i32, i16 = jnp.float32, jnp.bfloat16, jnp.int32, jnp.int16


def column(row):
    return jnp.broadcast_to(row, (LANES, LANES)).T


def merged(wide, first, n):
    return jnp.concatenate([wide[pl.ds(2 * first + s, n, stride=2), :] for s in range(SPECIES)], axis=1)


def step_kernel(n_dx, n_dy, dust_ref, cls_ref, ker_ref, export_ref, coef_ref, faces_ref, mig_ref, count_ref,
                next_ref, arrive_ref, dust, kernels, ext, coefs, wide, picked, outbound, ghosts, leave, updated,
                scaled_faces, scaled_exports, cls_wide, *rest):
    ids, exports = rest[:FACES * PARTS], rest[FACES * PARTS:FACES * PARTS + 4 * PICKS]
    load_sem, send_sem, recv_sem, ids_sem, own_sem, out_sem, leave_sem, arrive_sem = rest[FACES * PARTS + 4 * PICKS:]
    rows = dust_ref.shape[0]
    exported = export_ref.shape[1]
    cap = mig_ref.shape[0]
    count = n_dx * n_dy
    part_rows, pick_rows = rows // PARTS, exported // PICKS
    a, b = lax.axis_index("dx"), lax.axis_index("dy")
    me = a * n_dy + b

    def position(device):
        return (device // n_dy, lax.rem(device, n_dy))

    loads = [pltpu.make_async_copy(ker_ref, kernels, load_sem.at[0])]
    for n in range(rows // (2 * BLOCK)):
        part = pl.ds(n * 2 * BLOCK, 2 * BLOCK)
        loads.append(pltpu.make_async_copy(dust_ref.at[part], dust.at[part], load_sem.at[1 + n]))
    for copy in loads:
        copy.start()

    def greet(peer):
        pl.semaphore_signal(pltpu.get_barrier_semaphore(), inc=1, device_id=peer, device_id_type=MESH)

    for k in range(1, n_dy):
        greet((a, lax.rem(b + k, n_dy)))

    def greet_row(k, carry):
        other = lax.rem(a + k, n_dx)
        for peer in range(n_dy):
            greet((other, peer))
        return carry

    lax.fori_loop(1, n_dx, greet_row, 0)

    scaled_exports[...] = export_ref[...] * 2
    scaled_faces[...] = faces_ref[...] * 2
    lookups = []
    for k in range(4):
        for u in range(PICKS):
            n = k * PICKS + u
            lookups.append(pltpu.make_async_copy(
                scaled_exports.at[pl.ds(k, 1), pl.ds(u * pick_rows, pick_rows)], exports[n], ids_sem.at[n]))
    for f in range(FACES):
        for u in range(PARTS):
            n = f * PARTS + u
            lookups.append(pltpu.make_async_copy(
                scaled_faces.at[pl.ds(f, 1), pl.ds(u * part_rows, part_rows)], ids[n], ids_sem.at[4 * PICKS + n]))
    for copy in lookups:
        copy.start()
    for k in range(rows // LANES):
        cls_wide[k * LANES:(k + 1) * LANES, :] = column(cls_ref[k:k + 1, :])

    def substeps(s):
        weights = [
            jnp.concatenate([kernels[2 * p, s], kernels[2 * p + 1, s]], axis=1) for p in range(kernels.shape[0] // 2)
        ]

        def run(i, carry):
            firsts = [pl.multiple_of((2 * i + h) * BLOCK, BLOCK) for h in range(2)]
            groups = [cls_wide[pl.ds(first, BLOCK), :] for first in firsts]
            odd = [(group & 1) == 1 for group in groups]
            pairs = [(group >> 1).astype(i16) for group in groups]
            state = [dust[pl.ds(first, BLOCK), s * LANES:(s + 1) * LANES].astype(f32) for first in firsts]
            for substep in range(SUBSTEPS):
                for h in range(2):
                    operand = state[h].astype(bf16)
                    zero = jnp.zeros_like(operand)
                    spread = jnp.concatenate(
                        [jnp.where(pairs[h] == p, operand, zero) for p in range(len(weights))], axis=1)
                    both = jnp.dot(spread, jnp.concatenate(weights, axis=0), preferred_element_type=f32)
                    product = jnp.where(odd[h], both[:, LANES:], both[:, :LANES])
                    squares = jnp.sum(state[h] * state[h], axis=1, keepdims=True)
                    state[h] = state[h] + product * (squares / (LANES + squares))
            for h in range(2):
                ext[pl.ds(2 * firsts[h] + s, BLOCK, stride=2), :] = state[h].astype(bf16).astype(f32)
            return carry

        lax.fori_loop(0, rows // (2 * BLOCK), run, 0)

    peers = [
        (lax.rem(a + 1, n_dx), b),
        (lax.rem(a + n_dx - 1, n_dx), b),
        (a, lax.rem(b + 1, n_dy)),
        (a, lax.rem(b + n_dy - 1, n_dy)),
    ]

    def halo(s, k):
        place = pl.ds(k * exported, exported)
        return pltpu.make_async_remote_copy(
            src_ref=outbound.at[s, place],
            dst_ref=ghosts.at[s, place],
            send_sem=send_sem.at[s * 4 + k],
            recv_sem=recv_sem.at[s * 4 + k],
            device_id=peers[k],
            device_id_type=MESH,
        )

    for copy in loads:
        copy.wait()
    for s in range(SPECIES):
        substeps(s)
        if s == 0:
            for copy in lookups:
                copy.wait()
            pl.semaphore_wait(pltpu.get_barrier_semaphore(), count - 1)
        for k in (2, 3, 0, 1):

            def pick(i, carry):
                for v in range(PICK_UNROLL):
                    at = i * PICK_UNROLL + v
                    for u in range(PICKS):
                        row = exports[k * PICKS + u][0, at] + s
                        picked[pl.ds(u * pick_rows + at, 1), :] = ext[pl.ds(row, 1), :]
                return carry

            lax.fori_loop(0, pick_rows // PICK_UNROLL, pick, 0)

            def narrow(i, carry):
                first = pl.multiple_of(i * 256, 256)
                outbound[s, pl.ds(k * exported + first, 256), :] = picked[pl.ds(first, 256), :].astype(bf16)
                return carry

            lax.fori_loop(0, exported // 256, narrow, 0)
            halo(s, k).start()

    def spread(i, carry):
        first = pl.multiple_of(i * LANES, LANES)
        for f in range(FACES):
            weight = column(coef_ref[f:f + 1, pl.ds(first, LANES)])
            for half in range(2):
                coefs[pl.ds(2 * (f * rows + first) + half, LANES, stride=2), :] = weight
        return carry

    lax.fori_loop(0, rows // LANES, spread, 0)
    for s in range(SPECIES):
        for k in (0, 1, 2, 3):
            halo(s, k).wait()

            def widen(i, carry):
                first = pl.multiple_of(i * LANES, LANES)
                at = rows + k * exported + first
                ext[pl.ds(2 * at + s, LANES, stride=2), :] = ghosts[
                    s, pl.ds(k * exported + first, LANES), :].astype(f32)
                return carry

            lax.fori_loop(0, exported // LANES, widen, 0)

    def stay(i, carry):
        at = pl.multiple_of(i * UNROLL, UNROLL)
        for u in range(PARTS):
            first = pl.multiple_of(u * part_rows + at, UNROLL)
            for j in range(UNROLL):
                pair = 2 * (first + j)
                own = ext[pl.ds(pair, 2), :]
                total = own
                for f in range(FACES):
                    row = ids[f * PARTS + u][0, at + j]
                    total = total + coefs[pl.ds(2 * f * rows + pair, 2), :] * (ext[pl.ds(row, 2), :] - own)
                wide[pl.ds(pair, 2), :] = total
            updated[pl.ds(first, UNROLL), :] = merged(wide, first, UNROLL).astype(bf16)
        return carry

    lax.fori_loop(0, part_rows // UNROLL, stay, 0)
    out = pltpu.make_async_copy(updated, next_ref, out_sem)
    out.start()

    def place(domain):
        return pl.ds(pl.multiple_of(domain * cap, cap), cap)

    slot = lax.broadcasted_iota(i32, (cap, SPECIES * LANES), 0)

    def pack(domain):
        for j in range(cap):
            picked[pl.ds(2 * j, 2), :] = wide[pl.ds(2 * mig_ref[j, domain], 2), :]
        kept = jnp.clip(count_ref[0, domain] - slot, 0, 1).astype(f32)
        leave[place(domain), :] = (merged(picked, 0, cap) * kept).astype(bf16)

    def send(k, carry):
        domain = lax.rem(me + k, count)
        pack(domain)
        pltpu.make_async_remote_copy(
            src_ref=leave.at[place(domain)],
            dst_ref=arrive_ref.at[place(me)],
            send_sem=leave_sem,
            recv_sem=arrive_sem,
            device_id=position(domain),
            device_id_type=MESH,
        ).start()
        return carry

    lax.fori_loop(1, count, send, 0)
    pack(me)
    own = pltpu.make_async_copy(leave.at[place(me)], arrive_ref.at[place(me)], own_sem)
    own.start()
    own.wait()
    others = pl.ds(0, (count - 1) * cap)
    pltpu.make_async_copy(leave.at[others], leave.at[others], leave_sem).wait()
    pltpu.make_async_copy(arrive_ref.at[others], arrive_ref.at[others], arrive_sem).wait()
    out.wait()


def advance(dust, classes, kernels, export_ids, face_coef, faces, mig_ids, counts, n_dx, n_dy):
    rows, width = dust.shape
    sent = export_ids.shape[0] * export_ids.shape[1]
    moved = mig_ids.shape[0] * mig_ids.shape[1]
    vmem = pl.BlockSpec(memory_space=pltpu.VMEM)
    smem = pl.BlockSpec(memory_space=pltpu.SMEM)
    hbm = pl.BlockSpec(memory_space=pl.ANY)
    dma = pltpu.SemaphoreType.DMA
    return pl.pallas_call(
        functools.partial(step_kernel, n_dx, n_dy),
        in_specs=[hbm, vmem, hbm, vmem, vmem, vmem, smem, smem],
        out_specs=[hbm, hbm],
        out_shape=[jax.ShapeDtypeStruct((rows, width), bf16), jax.ShapeDtypeStruct((moved, width), bf16)],
        scratch_shapes=[
            pltpu.VMEM(dust.shape, bf16),
            pltpu.VMEM(kernels.shape, bf16),
            pltpu.VMEM((2 * (rows + sent), LANES), f32),
            pltpu.VMEM((2 * FACES * rows, LANES), f32),
            pltpu.VMEM((2 * rows, LANES), f32),
            pltpu.VMEM((export_ids.shape[1], LANES), f32),
            pltpu.VMEM((SPECIES, sent, LANES), bf16),
            pltpu.VMEM((SPECIES, sent, LANES), bf16),
            pltpu.VMEM((moved, width), bf16),
            pltpu.VMEM((rows, width), bf16),
            pltpu.VMEM(faces.shape, i32),
            pltpu.VMEM(export_ids.shape, i32),
            pltpu.VMEM((rows, LANES), i32),
            *[pltpu.SMEM((1, rows // PARTS), i32)] * (FACES * PARTS),
            *[pltpu.SMEM((1, export_ids.shape[1] // PICKS), i32)] * (4 * PICKS),
            dma((1 + rows // (2 * BLOCK),)), dma((8,)), dma((8,)), dma((FACES * PARTS + 4 * PICKS,)),
            dma, dma, dma, dma,
        ],
        compiler_params=pltpu.CompilerParams(
            vmem_limit_bytes=60 << 20, collective_id=0, has_side_effects=True),
        name="advance",
    )(dust, classes, kernels, export_ids, face_coef, faces, mig_ids, counts)


def hand_over_kernel(pieces, *refs):
    sources, targets, buffers, in_sem, out_sem = refs[:2], refs[2:4], refs[4:6], refs[6], refs[7]
    loads, stores = [], []
    for n in range(2):
        rows = sources[n].shape[0] // pieces
        for k in range(pieces):
            part = pl.ds(k * rows, rows)
            loads.append(pltpu.make_async_copy(sources[n].at[part], buffers[n].at[part], in_sem.at[n * pieces + k]))
            stores.append(pltpu.make_async_copy(buffers[n].at[part], targets[n].at[part], out_sem.at[n * pieces + k]))
    for load in loads:
        load.start()
    for load, store in zip(loads, stores):
        load.wait()
        store.start()
    for store in stores:
        store.wait()


def hand_over(*arrays):
    hbm = pl.BlockSpec(memory_space=pl.ANY)
    pieces = 4
    return pl.pallas_call(
        functools.partial(hand_over_kernel, pieces),
        in_specs=[hbm] * 2,
        out_specs=[hbm] * 2,
        out_shape=[jax.ShapeDtypeStruct(x.shape, x.dtype) for x in arrays],
        scratch_shapes=[
            *[pltpu.VMEM(x.shape, x.dtype) for x in arrays],
            pltpu.SemaphoreType.DMA((2 * pieces,)),
            pltpu.SemaphoreType.DMA((2 * pieces,)),
        ],
        name="hand_over",
    )(*arrays)


def body(n_dx, n_dy, dust, classes, kernels, export_ids, faces, face_coef, mig_ids, mig_counts):
    updated, arrivals = advance(
        dust, classes.reshape(-1, LANES), kernels, export_ids[0], face_coef, faces, mig_ids.T, mig_counts, n_dx, n_dy)
    return tuple(hand_over(updated, arrivals))


def solution(mesh):
    return jax.shard_map(
        functools.partial(body, mesh.shape["dx"], mesh.shape["dy"]),
        mesh=mesh,
        in_specs=(
            P(("dx", "dy"), None),
            P(("dx", "dy")),
            P(),
            P(("dx", "dy"), None, None),
            P(None, ("dx", "dy")),
            P(None, ("dx", "dy")),
            P(("dx", "dy"), None),
            P(("dx", "dy"), None),
        ),
        out_specs=(P(("dx", "dy"), None), P(("dx", "dy"), None)),
        check_vma=False,
    )
```

```python
import functools
import jax
import jax.numpy as jnp
from jax import lax
from jax.experimental import pallas as pl
from jax.experimental.pallas import tpu as pltpu
from jax.sharding import PartitionSpec as P

SUBSTEPS = 6
SPECIES = 2
LANES = 128
FACES = 6
BLOCK = 1024
PARTS = 1
UNROLL = 32
PICKS = 8
PICK_UNROLL = 8
MESH = pl.DeviceIdType.MESH
f32, bf16, i32, i16 = jnp.float32, jnp.bfloat16, jnp.int32, jnp.int16


def column(row):
    return jnp.broadcast_to(row, (LANES, LANES)).T


def merged(wide, first, n):
    return jnp.concatenate([wide[pl.ds(2 * first + s, n, stride=2), :] for s in range(SPECIES)], axis=1)


def step_kernel(n_dx, n_dy, dust_ref, cls_ref, ker_ref, export_ref, coef_ref, faces_ref, mig_ref, count_ref,
                next_ref, arrive_ref, dust, kernels, ext, coefs, wide, picked, outbound, ghosts, leave, updated,
                scaled_faces, scaled_exports, cls_wide, *rest):
    ids, exports = rest[:FACES * PARTS], rest[FACES * PARTS:FACES * PARTS + 4 * PICKS]
    load_sem, send_sem, recv_sem, ids_sem, own_sem, out_sem, leave_sem, arrive_sem = rest[FACES * PARTS + 4 * PICKS:]
    rows = dust_ref.shape[0]
    exported = export_ref.shape[1]
    cap = mig_ref.shape[0]
    count = n_dx * n_dy
    part_rows, pick_rows = rows // PARTS, exported // PICKS
    a, b = lax.axis_index("dx"), lax.axis_index("dy")
    me = a * n_dy + b

    def position(device):
        return (device // n_dy, lax.rem(device, n_dy))

    loads = [pltpu.make_async_copy(ker_ref, kernels, load_sem.at[0])]
    for n in range(rows // (2 * BLOCK)):
        part = pl.ds(n * 2 * BLOCK, 2 * BLOCK)
        loads.append(pltpu.make_async_copy(dust_ref.at[part], dust.at[part], load_sem.at[1 + n]))
    for copy in loads:
        copy.start()

    def greet(peer):
        pl.semaphore_signal(pltpu.get_barrier_semaphore(), inc=1, device_id=peer, device_id_type=MESH)

    for k in range(1, n_dy):
        greet((a, lax.rem(b + k, n_dy)))

    def greet_row(k, carry):
        other = lax.rem(a + k, n_dx)
        for peer in range(n_dy):
            greet((other, peer))
        return carry

    lax.fori_loop(1, n_dx, greet_row, 0)

    scaled_exports[...] = export_ref[...] * 2
    scaled_faces[...] = faces_ref[...] * 2
    lookups = []
    for k in range(4):
        for u in range(PICKS):
            n = k * PICKS + u
            lookups.append(pltpu.make_async_copy(
                scaled_exports.at[pl.ds(k, 1), pl.ds(u * pick_rows, pick_rows)], exports[n], ids_sem.at[n]))
    for f in range(FACES):
        for u in range(PARTS):
            n = f * PARTS + u
            lookups.append(pltpu.make_async_copy(
                scaled_faces.at[pl.ds(f, 1), pl.ds(u * part_rows, part_rows)], ids[n], ids_sem.at[4 * PICKS + n]))
    for copy in lookups:
        copy.start()
    for k in range(rows // LANES):
        cls_wide[k * LANES:(k + 1) * LANES, :] = column(cls_ref[k:k + 1, :])

    def substeps(s):
        weights = [
            jnp.concatenate([kernels[2 * p, s], kernels[2 * p + 1, s]], axis=1) for p in range(kernels.shape[0] // 2)
        ]

        def run(i, carry):
            firsts = [pl.multiple_of((2 * i + h) * BLOCK, BLOCK) for h in range(2)]
            groups = [cls_wide[pl.ds(first, BLOCK), :] for first in firsts]
            odd = [(group & 1) == 1 for group in groups]
            pairs = [(group >> 1).astype(i16) for group in groups]
            state = [dust[pl.ds(first, BLOCK), s * LANES:(s + 1) * LANES].astype(f32) for first in firsts]
            for substep in range(SUBSTEPS):
                for h in range(2):
                    operand = state[h].astype(bf16)
                    zero = jnp.zeros_like(operand)
                    spread = jnp.concatenate(
                        [jnp.where(pairs[h] == p, operand, zero) for p in range(len(weights))], axis=1)
                    both = jnp.dot(spread, jnp.concatenate(weights, axis=0), preferred_element_type=f32)
                    product = jnp.where(odd[h], both[:, LANES:], both[:, :LANES])
                    squares = jnp.sum(state[h] * state[h], axis=1, keepdims=True)
                    state[h] = state[h] + product * (squares / (LANES + squares))
            for h in range(2):
                ext[pl.ds(2 * firsts[h] + s, BLOCK, stride=2), :] = state[h].astype(bf16).astype(f32)
            return carry

        lax.fori_loop(0, rows // (2 * BLOCK), run, 0)

    peers = [
        (lax.rem(a + 1, n_dx), b),
        (lax.rem(a + n_dx - 1, n_dx), b),
        (a, lax.rem(b + 1, n_dy)),
        (a, lax.rem(b + n_dy - 1, n_dy)),
    ]

    def halo(s, k):
        place = pl.ds(k * exported, exported)
        return pltpu.make_async_remote_copy(
            src_ref=outbound.at[s, place],
            dst_ref=ghosts.at[s, place],
            send_sem=send_sem.at[s * 4 + k],
            recv_sem=recv_sem.at[s * 4 + k],
            device_id=peers[k],
            device_id_type=MESH,
        )

    for copy in loads:
        copy.wait()
    for s in range(SPECIES):
        substeps(s)
        if s == 0:
            for copy in lookups:
                copy.wait()
            pl.semaphore_wait(pltpu.get_barrier_semaphore(), count - 1)
        for k in (2, 3, 0, 1):

            def pick(i, carry):
                for v in range(PICK_UNROLL):
                    at = i * PICK_UNROLL + v
                    for u in range(PICKS):
                        row = exports[k * PICKS + u][0, at] + s
                        picked[pl.ds(u * pick_rows + at, 1), :] = ext[pl.ds(row, 1), :]
                return carry

            lax.fori_loop(0, pick_rows // PICK_UNROLL, pick, 0)

            def narrow(i, carry):
                first = pl.multiple_of(i * 256, 256)
                outbound[s, pl.ds(k * exported + first, 256), :] = picked[pl.ds(first, 256), :].astype(bf16)
                return carry

            lax.fori_loop(0, exported // 256, narrow, 0)
            halo(s, k).start()

    def spread(i, carry):
        first = pl.multiple_of(i * LANES, LANES)
        for f in range(FACES):
            weight = column(coef_ref[f:f + 1, pl.ds(first, LANES)])
            for half in range(2):
                coefs[pl.ds(2 * (f * rows + first) + half, LANES, stride=2), :] = weight
        return carry

    lax.fori_loop(0, rows // LANES, spread, 0)
    for s in range(SPECIES):
        for k in (0, 1, 2, 3):
            halo(s, k).wait()

            def widen(i, carry):
                first = pl.multiple_of(i * LANES, LANES)
                at = rows + k * exported + first
                ext[pl.ds(2 * at + s, LANES, stride=2), :] = ghosts[
                    s, pl.ds(k * exported + first, LANES), :].astype(f32)
                return carry

            lax.fori_loop(0, exported // LANES, widen, 0)

    def stay(i, carry):
        at = pl.multiple_of(i * UNROLL, UNROLL)
        for u in range(PARTS):
            first = pl.multiple_of(u * part_rows + at, UNROLL)
            for j in range(UNROLL):
                pair = 2 * (first + j)
                own = ext[pl.ds(pair, 2), :]
                total = own
                for f in range(FACES):
                    row = ids[f * PARTS + u][0, at + j]
                    total = total + coefs[pl.ds(2 * f * rows + pair, 2), :] * (ext[pl.ds(row, 2), :] - own)
                wide[pl.ds(pair, 2), :] = total
            updated[pl.ds(first, UNROLL), :] = merged(wide, first, UNROLL).astype(bf16)
        return carry

    lax.fori_loop(0, part_rows // UNROLL, stay, 0)
    out = pltpu.make_async_copy(updated, next_ref, out_sem)
    out.start()

    def place(domain):
        return pl.ds(pl.multiple_of(domain * cap, cap), cap)

    slot = lax.broadcasted_iota(i32, (cap, SPECIES * LANES), 0)

    def pack(domain):
        for j in range(cap):
            picked[pl.ds(2 * j, 2), :] = wide[pl.ds(2 * mig_ref[j, domain], 2), :]
        kept = jnp.clip(count_ref[0, domain] - slot, 0, 1).astype(f32)
        leave[place(domain), :] = (merged(picked, 0, cap) * kept).astype(bf16)

    def ship(domain):
        pack(domain)
        pltpu.make_async_remote_copy(
            src_ref=leave.at[place(domain)],
            dst_ref=arrive_ref.at[place(me)],
            send_sem=leave_sem,
            recv_sem=arrive_sem,
            device_id=position(domain),
            device_id_type=MESH,
        ).start()

    def send(k, carry):
        ship(lax.rem(me + count // 2 - k, count))
        ship(lax.rem(me + count // 2 + k, count))
        return carry

    ship(lax.rem(me + count // 2, count))
    lax.fori_loop(1, count // 2, send, 0)
    pack(me)
    own = pltpu.make_async_copy(leave.at[place(me)], arrive_ref.at[place(me)], own_sem)
    own.start()
    own.wait()
    others = pl.ds(0, (count - 1) * cap)
    pltpu.make_async_copy(leave.at[others], leave.at[others], leave_sem).wait()
    pltpu.make_async_copy(arrive_ref.at[others], arrive_ref.at[others], arrive_sem).wait()
    out.wait()


def advance(dust, classes, kernels, export_ids, face_coef, faces, mig_ids, counts, n_dx, n_dy):
    rows, width = dust.shape
    sent = export_ids.shape[0] * export_ids.shape[1]
    moved = mig_ids.shape[0] * mig_ids.shape[1]
    vmem = pl.BlockSpec(memory_space=pltpu.VMEM)
    smem = pl.BlockSpec(memory_space=pltpu.SMEM)
    hbm = pl.BlockSpec(memory_space=pl.ANY)
    dma = pltpu.SemaphoreType.DMA
    return pl.pallas_call(
        functools.partial(step_kernel, n_dx, n_dy),
        in_specs=[hbm, vmem, hbm, vmem, vmem, vmem, smem, smem],
        out_specs=[hbm, hbm],
        out_shape=[jax.ShapeDtypeStruct((rows, width), bf16), jax.ShapeDtypeStruct((moved, width), bf16)],
        scratch_shapes=[
            pltpu.VMEM(dust.shape, bf16),
            pltpu.VMEM(kernels.shape, bf16),
            pltpu.VMEM((2 * (rows + sent), LANES), f32),
            pltpu.VMEM((2 * FACES * rows, LANES), f32),
            pltpu.VMEM((2 * rows, LANES), f32),
            pltpu.VMEM((export_ids.shape[1], LANES), f32),
            pltpu.VMEM((SPECIES, sent, LANES), bf16),
            pltpu.VMEM((SPECIES, sent, LANES), bf16),
            pltpu.VMEM((moved, width), bf16),
            pltpu.VMEM((rows, width), bf16),
            pltpu.VMEM(faces.shape, i32),
            pltpu.VMEM(export_ids.shape, i32),
            pltpu.VMEM((rows, LANES), i32),
            *[pltpu.SMEM((1, rows // PARTS), i32)] * (FACES * PARTS),
            *[pltpu.SMEM((1, export_ids.shape[1] // PICKS), i32)] * (4 * PICKS),
            dma((1 + rows // (2 * BLOCK),)), dma((8,)), dma((8,)), dma((FACES * PARTS + 4 * PICKS,)),
            dma, dma, dma, dma,
        ],
        compiler_params=pltpu.CompilerParams(
            vmem_limit_bytes=60 << 20, collective_id=0, has_side_effects=True),
        name="advance",
    )(dust, classes, kernels, export_ids, face_coef, faces, mig_ids, counts)


def hand_over_kernel(pieces, *refs):
    sources, targets, buffers, in_sem, out_sem = refs[:2], refs[2:4], refs[4:6], refs[6], refs[7]
    loads, stores = [], []
    for n in range(2):
        rows = sources[n].shape[0] // pieces
        for k in range(pieces):
            part = pl.ds(k * rows, rows)
            loads.append(pltpu.make_async_copy(sources[n].at[part], buffers[n].at[part], in_sem.at[n * pieces + k]))
            stores.append(pltpu.make_async_copy(buffers[n].at[part], targets[n].at[part], out_sem.at[n * pieces + k]))
    for load in loads:
        load.start()
    for load, store in zip(loads, stores):
        load.wait()
        store.start()
    for store in stores:
        store.wait()


def hand_over(*arrays):
    hbm = pl.BlockSpec(memory_space=pl.ANY)
    pieces = 4
    return pl.pallas_call(
        functools.partial(hand_over_kernel, pieces),
        in_specs=[hbm] * 2,
        out_specs=[hbm] * 2,
        out_shape=[jax.ShapeDtypeStruct(x.shape, x.dtype) for x in arrays],
        scratch_shapes=[
            *[pltpu.VMEM(x.shape, x.dtype) for x in arrays],
            pltpu.SemaphoreType.DMA((2 * pieces,)),
            pltpu.SemaphoreType.DMA((2 * pieces,)),
        ],
        name="hand_over",
    )(*arrays)


def body(n_dx, n_dy, dust, classes, kernels, export_ids, faces, face_coef, mig_ids, mig_counts):
    updated, arrivals = advance(
        dust, classes.reshape(-1, LANES), kernels, export_ids[0], face_coef, faces, mig_ids.T, mig_counts, n_dx, n_dy)
    return tuple(hand_over(updated, arrivals))


def solution(mesh):
    return jax.shard_map(
        functools.partial(body, mesh.shape["dx"], mesh.shape["dy"]),
        mesh=mesh,
        in_specs=(
            P(("dx", "dy"), None),
            P(("dx", "dy")),
            P(),
            P(("dx", "dy"), None, None),
            P(None, ("dx", "dy")),
            P(None, ("dx", "dy")),
            P(("dx", "dy"), None),
            P(("dx", "dy"), None),
        ),
        out_specs=(P(("dx", "dy"), None), P(("dx", "dy"), None)),
        check_vma=False,
    )
```

```python
import functools
import jax
import jax.numpy as jnp
from jax import lax
from jax.experimental import pallas as pl
from jax.experimental.pallas import tpu as pltpu
from jax.sharding import PartitionSpec as P

SUBSTEPS = 6
SPECIES = 2
LANES = 128
FACES = 6
BLOCK = 1024
PARTS = 1
UNROLL = 64
PICKS = 8
PICK_UNROLL = 8
MESH = pl.DeviceIdType.MESH
f32, bf16, i32, i16 = jnp.float32, jnp.bfloat16, jnp.int32, jnp.int16


def column(row):
    return jnp.broadcast_to(row, (LANES, LANES)).T


def merged(wide, first, n):
    return jnp.concatenate([wide[pl.ds(2 * first + s, n, stride=2), :] for s in range(SPECIES)], axis=1)


def step_kernel(n_dx, n_dy, dust_ref, cls_ref, ker_ref, export_ref, coef_ref, faces_ref, mig_ref, count_ref,
                next_ref, arrive_ref, dust, kernels, ext, coefs, wide, picked, outbound, ghosts, leave, updated,
                scaled_faces, scaled_exports, cls_wide, *rest):
    ids, exports = rest[:FACES * PARTS], rest[FACES * PARTS:FACES * PARTS + 4 * PICKS]
    load_sem, send_sem, recv_sem, ids_sem, own_sem, out_sem, leave_sem, arrive_sem = rest[FACES * PARTS + 4 * PICKS:]
    rows = dust_ref.shape[0]
    exported = export_ref.shape[1]
    cap = mig_ref.shape[0]
    count = n_dx * n_dy
    part_rows, pick_rows = rows // PARTS, exported // PICKS
    a, b = lax.axis_index("dx"), lax.axis_index("dy")
    me = a * n_dy + b

    def position(device):
        return (device // n_dy, lax.rem(device, n_dy))

    loads = [pltpu.make_async_copy(ker_ref, kernels, load_sem.at[0])]
    for n in range(rows // (2 * BLOCK)):
        part = pl.ds(n * 2 * BLOCK, 2 * BLOCK)
        loads.append(pltpu.make_async_copy(dust_ref.at[part], dust.at[part], load_sem.at[1 + n]))
    for copy in loads:
        copy.start()

    def greet(peer):
        pl.semaphore_signal(pltpu.get_barrier_semaphore(), inc=1, device_id=peer, device_id_type=MESH)

    for k in range(1, n_dy):
        greet((a, lax.rem(b + k, n_dy)))

    def greet_row(k, carry):
        other = lax.rem(a + k, n_dx)
        for peer in range(n_dy):
            greet((other, peer))
        return carry

    lax.fori_loop(1, n_dx, greet_row, 0)

    scaled_exports[...] = export_ref[...] * 2
    scaled_faces[...] = faces_ref[...] * 2
    lookups = []
    for k in range(4):
        for u in range(PICKS):
            n = k * PICKS + u
            lookups.append(pltpu.make_async_copy(
                scaled_exports.at[pl.ds(k, 1), pl.ds(u * pick_rows, pick_rows)], exports[n], ids_sem.at[n]))
    for f in range(FACES):
        for u in range(PARTS):
            n = f * PARTS + u
            lookups.append(pltpu.make_async_copy(
                scaled_faces.at[pl.ds(f, 1), pl.ds(u * part_rows, part_rows)], ids[n], ids_sem.at[4 * PICKS + n]))
    for copy in lookups:
        copy.start()
    for k in range(rows // LANES):
        cls_wide[k * LANES:(k + 1) * LANES, :] = column(cls_ref[k:k + 1, :])

    def substeps(s):
        weights = [
            jnp.concatenate([kernels[2 * p, s], kernels[2 * p + 1, s]], axis=1) for p in range(kernels.shape[0] // 2)
        ]

        def run(i, carry):
            firsts = [pl.multiple_of((2 * i + h) * BLOCK, BLOCK) for h in range(2)]
            groups = [cls_wide[pl.ds(first, BLOCK), :] for first in firsts]
            odd = [(group & 1) == 1 for group in groups]
            pairs = [(group >> 1).astype(i16) for group in groups]
            state = [dust[pl.ds(first, BLOCK), s * LANES:(s + 1) * LANES].astype(f32) for first in firsts]
            for substep in range(SUBSTEPS):
                for h in range(2):
                    operand = state[h].astype(bf16)
                    zero = jnp.zeros_like(operand)
                    spread = jnp.concatenate(
                        [jnp.where(pairs[h] == p, operand, zero) for p in range(len(weights))], axis=1)
                    both = jnp.dot(spread, jnp.concatenate(weights, axis=0), preferred_element_type=f32)
                    product = jnp.where(odd[h], both[:, LANES:], both[:, :LANES])
                    squares = jnp.sum(state[h] * state[h], axis=1, keepdims=True)
                    state[h] = state[h] + product * (squares / (LANES + squares))
            for h in range(2):
                ext[pl.ds(2 * firsts[h] + s, BLOCK, stride=2), :] = state[h].astype(bf16).astype(f32)
            return carry

        lax.fori_loop(0, rows // (2 * BLOCK), run, 0)

    peers = [
        (lax.rem(a + 1, n_dx), b),
        (lax.rem(a + n_dx - 1, n_dx), b),
        (a, lax.rem(b + 1, n_dy)),
        (a, lax.rem(b + n_dy - 1, n_dy)),
    ]

    def halo(s, k):
        place = pl.ds(k * exported, exported)
        return pltpu.make_async_remote_copy(
            src_ref=outbound.at[s, place],
            dst_ref=ghosts.at[s, place],
            send_sem=send_sem.at[s * 4 + k],
            recv_sem=recv_sem.at[s * 4 + k],
            device_id=peers[k],
            device_id_type=MESH,
        )

    for copy in loads:
        copy.wait()
    for s in range(SPECIES):
        substeps(s)
        if s == 0:
            for copy in lookups:
                copy.wait()
            pl.semaphore_wait(pltpu.get_barrier_semaphore(), count - 1)
        for k in (2, 3, 0, 1):

            def pick(i, carry):
                for v in range(PICK_UNROLL):
                    at = i * PICK_UNROLL + v
                    for u in range(PICKS):
                        row = exports[k * PICKS + u][0, at] + s
                        picked[pl.ds(u * pick_rows + at, 1), :] = ext[pl.ds(row, 1), :]
                return carry

            lax.fori_loop(0, pick_rows // PICK_UNROLL, pick, 0)

            def narrow(i, carry):
                first = pl.multiple_of(i * 256, 256)
                outbound[s, pl.ds(k * exported + first, 256), :] = picked[pl.ds(first, 256), :].astype(bf16)
                return carry

            lax.fori_loop(0, exported // 256, narrow, 0)
            halo(s, k).start()

    def spread(i, carry):
        first = pl.multiple_of(i * LANES, LANES)
        for f in range(FACES):
            weight = column(coef_ref[f:f + 1, pl.ds(first, LANES)])
            for half in range(2):
                coefs[pl.ds(2 * (f * rows + first) + half, LANES, stride=2), :] = weight
        return carry

    lax.fori_loop(0, rows // LANES, spread, 0)
    for s in range(SPECIES):
        for k in (0, 1, 2, 3):
            halo(s, k).wait()

            def widen(i, carry):
                first = pl.multiple_of(i * LANES, LANES)
                at = rows + k * exported + first
                ext[pl.ds(2 * at + s, LANES, stride=2), :] = ghosts[
                    s, pl.ds(k * exported + first, LANES), :].astype(f32)
                return carry

            lax.fori_loop(0, exported // LANES, widen, 0)

    def stay(i, carry):
        at = pl.multiple_of(i * UNROLL, UNROLL)
        for u in range(PARTS):
            first = pl.multiple_of(u * part_rows + at, UNROLL)
            for j in range(UNROLL):
                pair = 2 * (first + j)
                own = ext[pl.ds(pair, 2), :]
                total = own
                for f in range(FACES):
                    row = ids[f * PARTS + u][0, at + j]
                    total = total + coefs[pl.ds(2 * f * rows + pair, 2), :] * (ext[pl.ds(row, 2), :] - own)
                wide[pl.ds(pair, 2), :] = total
            updated[pl.ds(first, UNROLL), :] = merged(wide, first, UNROLL).astype(bf16)
        return carry

    lax.fori_loop(0, part_rows // UNROLL, stay, 0)
    out = pltpu.make_async_copy(updated, next_ref, out_sem)
    out.start()

    def place(domain):
        return pl.ds(pl.multiple_of(domain * cap, cap), cap)

    slot = lax.broadcasted_iota(i32, (cap, SPECIES * LANES), 0)

    def pack(domain):
        for j in range(cap):
            picked[pl.ds(2 * j, 2), :] = wide[pl.ds(2 * mig_ref[j, domain], 2), :]
        kept = jnp.clip(count_ref[0, domain] - slot, 0, 1).astype(f32)
        leave[place(domain), :] = (merged(picked, 0, cap) * kept).astype(bf16)

    def ship(domain):
        pack(domain)
        pltpu.make_async_remote_copy(
            src_ref=leave.at[place(domain)],
            dst_ref=arrive_ref.at[place(me)],
            send_sem=leave_sem,
            recv_sem=arrive_sem,
            device_id=position(domain),
            device_id_type=MESH,
        ).start()

    def send(k, carry):
        ship(lax.rem(me + count // 2 - k, count))
        ship(lax.rem(me + count // 2 + k, count))
        return carry

    ship(lax.rem(me + count // 2, count))
    lax.fori_loop(1, count // 2, send, 0)
    pack(me)
    own = pltpu.make_async_copy(leave.at[place(me)], arrive_ref.at[place(me)], own_sem)
    own.start()
    own.wait()
    others = pl.ds(0, (count - 1) * cap)
    pltpu.make_async_copy(leave.at[others], leave.at[others], leave_sem).wait()
    pltpu.make_async_copy(arrive_ref.at[others], arrive_ref.at[others], arrive_sem).wait()
    out.wait()


def advance(dust, classes, kernels, export_ids, face_coef, faces, mig_ids, counts, n_dx, n_dy):
    rows, width = dust.shape
    sent = export_ids.shape[0] * export_ids.shape[1]
    moved = mig_ids.shape[0] * mig_ids.shape[1]
    vmem = pl.BlockSpec(memory_space=pltpu.VMEM)
    smem = pl.BlockSpec(memory_space=pltpu.SMEM)
    hbm = pl.BlockSpec(memory_space=pl.ANY)
    dma = pltpu.SemaphoreType.DMA
    return pl.pallas_call(
        functools.partial(step_kernel, n_dx, n_dy),
        in_specs=[hbm, vmem, hbm, vmem, vmem, vmem, smem, smem],
        out_specs=[hbm, hbm],
        out_shape=[jax.ShapeDtypeStruct((rows, width), bf16), jax.ShapeDtypeStruct((moved, width), bf16)],
        scratch_shapes=[
            pltpu.VMEM(dust.shape, bf16),
            pltpu.VMEM(kernels.shape, bf16),
            pltpu.VMEM((2 * (rows + sent), LANES), f32),
            pltpu.VMEM((2 * FACES * rows, LANES), f32),
            pltpu.VMEM((2 * rows, LANES), f32),
            pltpu.VMEM((export_ids.shape[1], LANES), f32),
            pltpu.VMEM((SPECIES, sent, LANES), bf16),
            pltpu.VMEM((SPECIES, sent, LANES), bf16),
            pltpu.VMEM((moved, width), bf16),
            pltpu.VMEM((rows, width), bf16),
            pltpu.VMEM(faces.shape, i32),
            pltpu.VMEM(export_ids.shape, i32),
            pltpu.VMEM((rows, LANES), i32),
            *[pltpu.SMEM((1, rows // PARTS), i32)] * (FACES * PARTS),
            *[pltpu.SMEM((1, export_ids.shape[1] // PICKS), i32)] * (4 * PICKS),
            dma((1 + rows // (2 * BLOCK),)), dma((8,)), dma((8,)), dma((FACES * PARTS + 4 * PICKS,)),
            dma, dma, dma, dma,
        ],
        compiler_params=pltpu.CompilerParams(
            vmem_limit_bytes=60 << 20, collective_id=0, has_side_effects=True),
        name="advance",
    )(dust, classes, kernels, export_ids, face_coef, faces, mig_ids, counts)


def hand_over_kernel(pieces, *refs):
    sources, targets, buffers, in_sem, out_sem = refs[:2], refs[2:4], refs[4:6], refs[6], refs[7]
    loads, stores = [], []
    for n in range(2):
        rows = sources[n].shape[0] // pieces
        for k in range(pieces):
            part = pl.ds(k * rows, rows)
            loads.append(pltpu.make_async_copy(sources[n].at[part], buffers[n].at[part], in_sem.at[n * pieces + k]))
            stores.append(pltpu.make_async_copy(buffers[n].at[part], targets[n].at[part], out_sem.at[n * pieces + k]))
    for load in loads:
        load.start()
    for load, store in zip(loads, stores):
        load.wait()
        store.start()
    for store in stores:
        store.wait()


def hand_over(*arrays):
    hbm = pl.BlockSpec(memory_space=pl.ANY)
    pieces = 4
    return pl.pallas_call(
        functools.partial(hand_over_kernel, pieces),
        in_specs=[hbm] * 2,
        out_specs=[hbm] * 2,
        out_shape=[jax.ShapeDtypeStruct(x.shape, x.dtype) for x in arrays],
        scratch_shapes=[
            *[pltpu.VMEM(x.shape, x.dtype) for x in arrays],
            pltpu.SemaphoreType.DMA((2 * pieces,)),
            pltpu.SemaphoreType.DMA((2 * pieces,)),
        ],
        name="hand_over",
    )(*arrays)


def body(n_dx, n_dy, dust, classes, kernels, export_ids, faces, face_coef, mig_ids, mig_counts):
    updated, arrivals = advance(
        dust, classes.reshape(-1, LANES), kernels, export_ids[0], face_coef, faces, mig_ids.T, mig_counts, n_dx, n_dy)
    return tuple(hand_over(updated, arrivals))


def solution(mesh):
    return jax.shard_map(
        functools.partial(body, mesh.shape["dx"], mesh.shape["dy"]),
        mesh=mesh,
        in_specs=(
            P(("dx", "dy"), None),
            P(("dx", "dy")),
            P(),
            P(("dx", "dy"), None, None),
            P(None, ("dx", "dy")),
            P(None, ("dx", "dy")),
            P(("dx", "dy"), None),
            P(("dx", "dy"), None),
        ),
        out_specs=(P(("dx", "dy"), None), P(("dx", "dy"), None)),
        check_vma=False,
    )
```

```python
import functools
import jax
import jax.numpy as jnp
from jax import lax
from jax.experimental import pallas as pl
from jax.experimental.pallas import tpu as pltpu
from jax.sharding import PartitionSpec as P

SUBSTEPS = 6
SPECIES = 2
LANES = 128
FACES = 6
BLOCK = 1024
SPARE = 16
PARTS = 1
UNROLL = 64
PICKS = 8
PICK_UNROLL = 8
MESH = pl.DeviceIdType.MESH
f32, bf16, i32, i16 = jnp.float32, jnp.bfloat16, jnp.int32, jnp.int16


def column(row):
    return jnp.broadcast_to(row, (LANES, LANES)).T


def merged(wide, first, n):
    return jnp.concatenate([wide[pl.ds(2 * first + s, n, stride=2), :] for s in range(SPECIES)], axis=1)


def step_kernel(n_dx, n_dy, dust_ref, cls_ref, ker_ref, export_ref, coef_ref, faces_ref, mig_ref, count_ref,
                next_ref, arrive_ref, dust, kernels, ext, coefs, wide, picked, outbound, ghosts, leave, updated,
                scaled_faces, scaled_exports, cls_wide, *rest):
    ids, exports = rest[:FACES * PARTS], rest[FACES * PARTS:FACES * PARTS + 4 * PICKS]
    load_sem, send_sem, recv_sem, ids_sem, own_sem, out_sem, leave_sem, arrive_sem = rest[FACES * PARTS + 4 * PICKS:]
    rows = dust_ref.shape[0]
    exported = export_ref.shape[1]
    cap = mig_ref.shape[0]
    count = n_dx * n_dy
    part_rows, pick_rows = rows // PARTS, exported // PICKS
    a, b = lax.axis_index("dx"), lax.axis_index("dy")
    me = a * n_dy + b

    def position(device):
        return (device // n_dy, lax.rem(device, n_dy))

    loads = [pltpu.make_async_copy(ker_ref, kernels, load_sem.at[0])]
    for n in range(rows // (2 * BLOCK)):
        part = pl.ds(n * 2 * BLOCK, 2 * BLOCK)
        loads.append(pltpu.make_async_copy(dust_ref.at[part], dust.at[part], load_sem.at[1 + n]))
    for copy in loads:
        copy.start()

    def greet(peer):
        pl.semaphore_signal(pltpu.get_barrier_semaphore(), inc=1, device_id=peer, device_id_type=MESH)

    for k in range(1, n_dy):
        greet((a, lax.rem(b + k, n_dy)))

    def greet_row(k, carry):
        other = lax.rem(a + k, n_dx)
        for peer in range(n_dy):
            greet((other, peer))
        return carry

    lax.fori_loop(1, n_dx, greet_row, 0)

    scaled_exports[...] = export_ref[...] * 2
    scaled_faces[...] = faces_ref[...] * 2
    lookups = []
    for k in range(4):
        for u in range(PICKS):
            n = k * PICKS + u
            lookups.append(pltpu.make_async_copy(
                scaled_exports.at[pl.ds(k, 1), pl.ds(u * pick_rows, pick_rows)], exports[n], ids_sem.at[n]))
    for f in range(FACES):
        for u in range(PARTS):
            n = f * PARTS + u
            lookups.append(pltpu.make_async_copy(
                scaled_faces.at[pl.ds(f, 1), pl.ds(u * part_rows, part_rows)], ids[n], ids_sem.at[4 * PICKS + n]))
    for copy in lookups:
        copy.start()
    for k in range(rows // LANES):
        cls_wide[k * LANES:(k + 1) * LANES, :] = column(cls_ref[k:k + 1, :])

    def substeps(s):
        weights = [
            jnp.concatenate([kernels[2 * p, s], kernels[2 * p + 1, s]], axis=1) for p in range(kernels.shape[0] // 2)
        ]

        def run(i, carry):
            firsts = [pl.multiple_of((2 * i + h) * BLOCK, BLOCK) for h in range(2)]
            groups = [cls_wide[pl.ds(first, BLOCK), :] for first in firsts]
            odd = [(group & 1) == 1 for group in groups]
            pairs = [(group >> 1).astype(i16) for group in groups]
            state = [dust[pl.ds(first, BLOCK), s * LANES:(s + 1) * LANES].astype(f32) for first in firsts]
            for substep in range(SUBSTEPS):
                for h in range(2):
                    operand = state[h].astype(bf16)
                    zero = jnp.zeros_like(operand)
                    spread = jnp.concatenate(
                        [jnp.where(pairs[h] == p, operand, zero) for p in range(len(weights))], axis=1)
                    both = jnp.dot(spread, jnp.concatenate(weights, axis=0), preferred_element_type=f32)
                    product = jnp.where(odd[h], both[:, LANES:], both[:, :LANES])
                    squares = jnp.sum(state[h] * state[h], axis=1, keepdims=True)
                    state[h] = state[h] + product * (squares / (LANES + squares))
            for h in range(2):
                ext[pl.ds(2 * firsts[h] + s, BLOCK, stride=2), :] = state[h].astype(bf16).astype(f32)
            return carry

        lax.fori_loop(0, rows // (2 * BLOCK), run, 0)

    peers = [
        (lax.rem(a + 1, n_dx), b),
        (lax.rem(a + n_dx - 1, n_dx), b),
        (a, lax.rem(b + 1, n_dy)),
        (a, lax.rem(b + n_dy - 1, n_dy)),
    ]

    def halo(s, k):
        place = pl.ds(k * exported, exported)
        return pltpu.make_async_remote_copy(
            src_ref=outbound.at[s, place],
            dst_ref=ghosts.at[s, place],
            send_sem=send_sem.at[s * 4 + k],
            recv_sem=recv_sem.at[s * 4 + k],
            device_id=peers[k],
            device_id_type=MESH,
        )

    for copy in loads:
        copy.wait()
    for s in range(SPECIES):
        substeps(s)
        if s == 0:
            for copy in lookups:
                copy.wait()
            pl.semaphore_wait(pltpu.get_barrier_semaphore(), count - 1)
        for k in (2, 3, 0, 1):

            def pick(i, carry):
                for v in range(PICK_UNROLL):
                    at = i * PICK_UNROLL + v
                    for u in range(PICKS):
                        row = exports[k * PICKS + u][0, at] + s
                        picked[pl.ds(u * pick_rows + at, 1), :] = ext[pl.ds(row, 1), :]
                return carry

            lax.fori_loop(0, pick_rows // PICK_UNROLL, pick, 0)

            def narrow(i, carry):
                first = pl.multiple_of(i * 256, 256)
                outbound[s, pl.ds(k * exported + first, 256), :] = picked[pl.ds(first, 256), :].astype(bf16)
                return carry

            lax.fori_loop(0, exported // 256, narrow, 0)
            halo(s, k).start()

    def spread(i, carry):
        first = pl.multiple_of(i * LANES, LANES)
        for f in range(FACES):
            weight = column(coef_ref[f:f + 1, pl.ds(first, LANES)])
            for half in range(2):
                coefs[pl.ds(2 * (f * rows + first) + half, LANES, stride=2), :] = weight
        return carry

    lax.fori_loop(0, rows // LANES, spread, 0)
    for s in range(SPECIES):
        for k in (0, 1, 2, 3):
            halo(s, k).wait()

            def widen(i, carry):
                first = pl.multiple_of(i * LANES, LANES)
                at = rows + k * exported + first
                ext[pl.ds(2 * at + s, LANES, stride=2), :] = ghosts[
                    s, pl.ds(k * exported + first, LANES), :].astype(f32)
                return carry

            lax.fori_loop(0, exported // LANES, widen, 0)

    def stay(i, carry):
        at = pl.multiple_of(i * UNROLL, UNROLL)
        for u in range(PARTS):
            first = pl.multiple_of(u * part_rows + at, UNROLL)
            for j in range(UNROLL):
                pair = 2 * (first + j)
                own = ext[pl.ds(pair, 2), :]
                total = own
                for f in range(FACES):
                    row = ids[f * PARTS + u][0, at + j]
                    total = total + coefs[pl.ds(2 * f * rows + pair, 2), :] * (ext[pl.ds(row, 2), :] - own)
                wide[pl.ds(pair, 2), :] = total
            updated[pl.ds(first, UNROLL), :] = merged(wide, first, UNROLL).astype(bf16)
        return carry

    lax.fori_loop(0, part_rows // UNROLL, stay, 0)
    out = pltpu.make_async_copy(updated, next_ref, out_sem)
    out.start()

    def place(domain):
        return pl.ds(pl.multiple_of(domain * cap, cap), cap)

    slot = lax.broadcasted_iota(i32, (cap, SPECIES * LANES), 0)

    def pack(domain):
        for j in range(cap):
            picked[pl.ds(2 * j, 2), :] = wide[pl.ds(2 * mig_ref[j, domain], 2), :]
        kept = jnp.clip(count_ref[0, domain] - slot, 0, 1).astype(f32)
        leave[place(domain), :] = (merged(picked, 0, cap) * kept).astype(bf16)

    def ship(domain):
        pack(domain)
        pltpu.make_async_remote_copy(
            src_ref=leave.at[place(domain)],
            dst_ref=arrive_ref.at[place(me)],
            send_sem=leave_sem,
            recv_sem=arrive_sem,
            device_id=position(domain),
            device_id_type=MESH,
        ).start()

    def send(k, carry):
        ship(lax.rem(me + count // 2 - k, count))
        ship(lax.rem(me + count // 2 + k, count))
        return carry

    ship(lax.rem(me + count // 2, count))
    lax.fori_loop(1, count // 2, send, 0)
    pack(me)
    own = pltpu.make_async_copy(leave.at[place(me)], arrive_ref.at[place(me)], own_sem)
    own.start()
    own.wait()
    others = pl.ds(0, (count - 1) * cap)
    pltpu.make_async_copy(leave.at[others], leave.at[others], leave_sem).wait()
    pltpu.make_async_copy(arrive_ref.at[others], arrive_ref.at[others], arrive_sem).wait()
    out.wait()


def advance(dust, classes, kernels, export_ids, face_coef, faces, mig_ids, counts, n_dx, n_dy):
    rows, width = dust.shape
    sent = export_ids.shape[0] * export_ids.shape[1]
    moved = mig_ids.shape[0] * mig_ids.shape[1]
    vmem = pl.BlockSpec(memory_space=pltpu.VMEM)
    smem = pl.BlockSpec(memory_space=pltpu.SMEM)
    hbm = pl.BlockSpec(memory_space=pl.ANY)
    dma = pltpu.SemaphoreType.DMA
    return pl.pallas_call(
        functools.partial(step_kernel, n_dx, n_dy),
        in_specs=[hbm, vmem, hbm, vmem, vmem, vmem, smem, smem],
        out_specs=[hbm, hbm],
        out_shape=[jax.ShapeDtypeStruct((rows, width), bf16), jax.ShapeDtypeStruct((moved, width), bf16)],
        scratch_shapes=[
            pltpu.VMEM(dust.shape, bf16),
            pltpu.VMEM(kernels.shape, bf16),
            pltpu.VMEM((2 * (rows + sent) + SPARE, LANES), f32),
            pltpu.VMEM((2 * FACES * rows + SPARE, LANES), f32),
            pltpu.VMEM((2 * rows + SPARE, LANES), f32),
            pltpu.VMEM((export_ids.shape[1] + SPARE, LANES), f32),
            pltpu.VMEM((SPECIES, sent, LANES), bf16),
            pltpu.VMEM((SPECIES, sent, LANES), bf16),
            pltpu.VMEM((moved, width), bf16),
            pltpu.VMEM((rows, width), bf16),
            pltpu.VMEM(faces.shape, i32),
            pltpu.VMEM(export_ids.shape, i32),
            pltpu.VMEM((rows, LANES), i32),
            *[pltpu.SMEM((1, rows // PARTS), i32)] * (FACES * PARTS),
            *[pltpu.SMEM((1, export_ids.shape[1] // PICKS), i32)] * (4 * PICKS),
            dma((1 + rows // (2 * BLOCK),)), dma((8,)), dma((8,)), dma((FACES * PARTS + 4 * PICKS,)),
            dma, dma, dma, dma,
        ],
        compiler_params=pltpu.CompilerParams(
            vmem_limit_bytes=60 << 20, collective_id=0, has_side_effects=True),
        name="advance",
    )(dust, classes, kernels, export_ids, face_coef, faces, mig_ids, counts)


def hand_over_kernel(pieces, *refs):
    sources, targets, buffers, in_sem, out_sem = refs[:2], refs[2:4], refs[4:6], refs[6], refs[7]
    loads, stores = [], []
    for n in range(2):
        rows = sources[n].shape[0] // pieces
        for k in range(pieces):
            part = pl.ds(k * rows, rows)
            loads.append(pltpu.make_async_copy(sources[n].at[part], buffers[n].at[part], in_sem.at[n * pieces + k]))
            stores.append(pltpu.make_async_copy(buffers[n].at[part], targets[n].at[part], out_sem.at[n * pieces + k]))
    for load in loads:
        load.start()
    for load, store in zip(loads, stores):
        load.wait()
        store.start()
    for store in stores:
        store.wait()


def hand_over(*arrays):
    hbm = pl.BlockSpec(memory_space=pl.ANY)
    pieces = 4
    return pl.pallas_call(
        functools.partial(hand_over_kernel, pieces),
        in_specs=[hbm] * 2,
        out_specs=[hbm] * 2,
        out_shape=[jax.ShapeDtypeStruct(x.shape, x.dtype) for x in arrays],
        scratch_shapes=[
            *[pltpu.VMEM(x.shape, x.dtype) for x in arrays],
            pltpu.SemaphoreType.DMA((2 * pieces,)),
            pltpu.SemaphoreType.DMA((2 * pieces,)),
        ],
        name="hand_over",
    )(*arrays)


def body(n_dx, n_dy, dust, classes, kernels, export_ids, faces, face_coef, mig_ids, mig_counts):
    updated, arrivals = advance(
        dust, classes.reshape(-1, LANES), kernels, export_ids[0], face_coef, faces, mig_ids.T, mig_counts, n_dx, n_dy)
    return tuple(hand_over(updated, arrivals))


def solution(mesh):
    return jax.shard_map(
        functools.partial(body, mesh.shape["dx"], mesh.shape["dy"]),
        mesh=mesh,
        in_specs=(
            P(("dx", "dy"), None),
            P(("dx", "dy")),
            P(),
            P(("dx", "dy"), None, None),
            P(None, ("dx", "dy")),
            P(None, ("dx", "dy")),
            P(("dx", "dy"), None),
            P(("dx", "dy"), None),
        ),
        out_specs=(P(("dx", "dy"), None), P(("dx", "dy"), None)),
        check_vma=False,
    )
```
